512 devices in a mesh: gx: 8 (over z), gy: 16 (over y_hi, x, core), gz: 4 (over y_lo).
Axes of the slice: x: 4, y: 8 (y_hi: 2, y_lo: 4; y = y_hi * 4 + y_lo), z: 8, core: 2. Of those that a mesh axis runs over, the one named last changes fastest.
Arguments:
- field: bfloat16 [64, 32, 256, 1024], P(None, 'gz', 'gy', 'gx'), may hold values from -8 to 8
- conv_first: bfloat16 [3, 3, 3, 64, 128], replicated, may hold values from -0.15625 to 0.15625
- norm_gain: float32 [128], replicated, may hold values from 0.5 to 1.5
- norm_shift: float32 [128], replicated, may hold values from -3 to 3
- conv_second: bfloat16 [3, 3, 3, 128, 128], replicated, may hold values from -0.109375 to 0.109375
Outputs:
- result: bfloat16 [128, 16, 128, 512], P(None, 'gz', 'gy', 'gx')
The draws below stay inside these ranges and needn't reach their ends.
All inputs are finite; a program needn't handle non-finite values.
Results may differ from the reference program's by a relative error of at most 0.0017.
The reference program's roundings to bfloat16 on the way (of `activation`) count: a program that leaves them out, or rounds other values in their place, can miss the bound.
Values may be sent and summed in bfloat16 or wider, within the bound.
A program may use at most 128 MiB of HBM per device.

```python
import jax
import jax.numpy as jnp
from jax import lax

CIN = 64
C = 128
NEWTON = 5
NX = 1024
NY = 256
NZ = 32


def draw_field(key, part):
    key_one = jax.random.fold_in(key, 11)
    zpos = jnp.arange(NZ, dtype=jnp.float32) / NZ
    ypos = jnp.arange(NY, dtype=jnp.float32) / NY
    xpos = jnp.arange(NX, dtype=jnp.float32) / NX
    ramp = zpos[:, None, None] + ypos[None, :, None] + xpos[None, None, :]
    wider = (CIN, NZ + 1, NY + 1, NX + 1)
    samples = jax.random.normal(key_one, wider, jnp.float32)
    along_x = samples[:, :, :, 1:] + samples[:, :, :, :-1]
    along_y = along_x[:, :, 1:, :] + along_x[:, :, :-1, :]
    along_z = along_y[:, 1:, :, :] + along_y[:, :-1, :, :]
    smooth = along_z * 0.35355339
    amplitude = jnp.exp(0.5 * ramp * jnp.log(3.0))
    values = smooth * amplitude[None]
    return jnp.clip(values, -8.0, 8.0).astype(jnp.bfloat16)


def gaussian(rng, shape, deviation, bound, held_as=jnp.bfloat16):
    return jnp.clip(deviation * jax.random.normal(rng, shape, jnp.float32), -bound, bound).astype(held_as)


def setup_inputs(seed: int = 0) -> dict:
    streams_of = jax.random.split(jax.random.key(seed), 6)
    return {
        "field": draw_field(jax.random.fold_in(streams_of[5], 71), 0),
        "conv_first": gaussian(streams_of[1], (3, 3, 3, CIN, C), (27 * CIN) ** -0.5, 0.15625),
        "norm_gain": jnp.clip(1.0 + 0.1 * jax.random.normal(streams_of[2], (C,), jnp.float32), 0.5, 1.5),
        "norm_shift": gaussian(streams_of[3], (C,), 0.5, 3.0, jnp.float32),
        "conv_second": gaussian(streams_of[4], (3, 3, 3, C, C), (27 * C) ** -0.5, 0.109375),
    }


epsilon = 1e-05
leak_slope = 0.2

def strided_first(field, kernel):
    depth = field.shape[1] // 2
    height = field.shape[2] // 2
    width = field.shape[3] // 2
    padded = jnp.pad(field, ((0, 0), (1, 0), (1, 0), (1, 0)))
    kernel_wide = kernel.astype(jnp.float32)

    def plane(index_value):
        slab = lax.dynamic_slice_in_dim(padded, (2 * index_value).astype(jnp.int32), 3, axis=1)
        total = jnp.zeros((kernel.shape[4], height, width), jnp.float32)
        for tap_z in range(3):
            for tap_y in range(3):
                for tap_x in range(3):
                    piece = slab[:, tap_z, tap_y:tap_y + 2 * height - 1:2, tap_x:tap_x + 2 * width - 1:2].astype(jnp.float32)
                    total = total + jnp.einsum('io,iyx->oyx', kernel_wide[tap_z, tap_y, tap_x], piece, precision=lax.Precision.HIGHEST)
        return total
    planes = lax.map(plane, jnp.arange(depth, dtype=jnp.int32))
    return jnp.transpose(planes, (1, 0, 2, 3))

def same_second(volume, kernel):
    depth, height, width = (volume.shape[1], volume.shape[2], volume.shape[3])
    padded = jnp.pad(volume, ((0, 0), (1, 1), (1, 1), (1, 1)))
    kernel_wide = kernel.astype(jnp.float32)

    def plane(index_value):
        slab = lax.dynamic_slice_in_dim(padded, index_value.astype(jnp.int32), 3, axis=1)
        total = jnp.zeros((kernel.shape[4], height, width), jnp.float32)
        for tap_z in range(3):
            for tap_y in range(3):
                for tap_x in range(3):
                    piece = slab[:, tap_z, tap_y:tap_y + height, tap_x:tap_x + width].astype(jnp.float32)
                    total = total + jnp.einsum('io,iyx->oyx', kernel_wide[tap_z, tap_y, tap_x], piece, precision=lax.Precision.HIGHEST)
        return total.astype(jnp.bfloat16)
    planes = lax.map(plane, jnp.arange(depth, dtype=jnp.int32))
    return jnp.transpose(planes, (1, 0, 2, 3))

def newton_whitener(covariance):
    trace_value = jnp.trace(covariance, axis1=1, axis2=2)
    scaled = covariance / trace_value[:, None, None]
    identity = jnp.broadcast_to(jnp.eye(covariance.shape[-1], dtype=covariance.dtype), covariance.shape)
    newton_mat = identity
    for repeat in range(NEWTON):
        square = jnp.einsum('gij,gjk->gik', newton_mat, newton_mat, precision=lax.Precision.HIGHEST)
        cubed = jnp.einsum('gij,gjk->gik', square, newton_mat, precision=lax.Precision.HIGHEST)
        newton_mat = 1.5 * newton_mat - 0.5 * jnp.einsum('gij,gjk->gik', cubed, scaled, precision=lax.Precision.HIGHEST)
    return newton_mat / jnp.sqrt(trace_value)[:, None, None]

def whiten(block, average, whitener, norm_gain, norm_shift):
    shape = block.shape
    grouped = block.reshape(2, shape[0] // 2, -1) - average[:, :, None]
    mixed = jnp.einsum('gij,gjm->gim', whitener, grouped, precision=lax.Precision.HIGHEST).reshape(shape)
    scaled = mixed * norm_gain[:, None, None, None] + norm_shift[:, None, None, None]
    return jnp.where(scaled >= 0, scaled, leak_slope * scaled).astype(jnp.bfloat16)

def reference(field, conv_first, norm_gain, norm_shift, conv_second):
    features = strided_first(field, conv_first)
    channels = features.shape[0]
    grouped = features.reshape(2, channels // 2, -1)
    average = lax.optimization_barrier(jnp.mean(grouped, axis=2))
    centered = grouped - average[:, :, None]
    covariance = jnp.einsum('gim,gjm->gij', centered, centered, precision=lax.Precision.HIGHEST) / centered.shape[2]
    covariance = covariance + epsilon * jnp.eye(channels // 2, dtype=covariance.dtype)[None]
    whitener = newton_whitener(covariance)
    activation = whiten(features, average, whitener, norm_gain, norm_shift)
    return same_second(activation, conv_second)
```

```python
import functools

import jax
import jax.numpy as jnp
from jax import lax
from jax.experimental import pallas as pl
from jax.experimental.pallas import tpu as pltpu
from jax.sharding import PartitionSpec as P

NEWTON = 5
EPSILON = 1e-05
LEAK = 0.2
AXES = ("gx", "gy", "gz")
MESH = pl.DeviceIdType.MESH
HIGHEST = lax.Precision.HIGHEST
f32 = jnp.float32
bf16 = jnp.bfloat16


def iota(shape, dim):
    return lax.broadcasted_iota(jnp.int32, shape, dim)


def dot(a, b, precision=None):
    return lax.dot_general(
        a, b, (((1,), (0,)), ((), ())), preferred_element_type=f32, precision=precision
    )


def dot_nt(a, b, precision=None):
    return lax.dot_general(
        a, b, (((1,), (1,)), ((), ())), preferred_element_type=f32, precision=precision
    )


def dot_tn(a, b, precision=None):
    return lax.dot_general(
        a, b, (((0,), (0,)), ((), ())), preferred_element_type=f32, precision=precision
    )


def diagonal_blocks(square):
    half = square.shape[0] // 2
    lane = iota((half, 2 * half), 1)
    return jnp.where(lane < half, square[:half], square[half:])


def split_rows(sel, tile):
    return dot_nt(sel, tile)


def features_kernel(
    sizes,
    field_ref,
    w_ref,
    feat_ref,
    rim_ref,
    mom_ref,
    mean_ref,
    halo,
    rows,
    taps,
    edge_out,
    edge_in,
    stage,
    part,
    outer,
    mine,
    send_in,
    recv_in,
    send_out,
    recv_out,
    send_ar,
    recv_ar,
):
    nx, ny, nz = sizes
    gx, gy, gz = (lax.axis_index(a) for a in AXES)
    group = ny // 2
    rank = lax.rem(gy, group)
    y_hi = gy // group
    column = y_hi * nz + gz
    columns = 2 * nz

    def shifted(dx, dy, dz):
        ok = []
        if dx:
            ok.append(gx < nx - 1 if dx > 0 else gx > 0)
        if dy:
            ok.append(gy < ny - 1 if dy > 0 else gy > 0)
        if dz:
            ok.append(gz < nz - 1 if dz > 0 else gz > 0)
        there = functools.reduce(jnp.logical_and, ok)
        return there, (
            jnp.clip(gx + dx, 0, nx - 1),
            jnp.clip(gy + dy, 0, ny - 1),
            jnp.clip(gz + dz, 0, nz - 1),
        )

    def remote(src, dst, send, recv, device):
        return pltpu.make_async_remote_copy(
            src_ref=src, dst_ref=dst, send_sem=send, recv_sem=recv, device_id=device, device_id_type=MESH
        )

    rim_ref_zero = jnp.zeros(edge_in.shape, f32)
    edge_in[...] = rim_ref_zero
    own = pltpu.make_async_copy(field_ref, halo.at[:, 1:, 1:], send_in.at[7])
    own.start()
    barrier = pltpu.get_barrier_semaphore()
    ups = [(1, 0, 0), (0, 1, 0), (0, 0, 1), (1, 1, 0), (1, 0, 1), (0, 1, 1), (1, 1, 1)]
    expected = jnp.int32(group - 1 + nx - 1 + columns - 1)
    for up in ups:
        below, device = shifted(*(-v for v in up))

        @pl.when(below)
        def _():
            pl.semaphore_signal(barrier, inc=1, device_id=device, device_id_type=MESH)

        above, _ = shifted(*up)
        expected = expected + above.astype(jnp.int32)
    for axis in range(3):
        for sign in (-1, 1):
            there, device = shifted(*(sign if a == axis else 0 for a in range(3)))

            @pl.when(there)
            def _():
                pl.semaphore_signal(barrier, inc=1, device_id=device, device_id_type=MESH)

            expected = expected + there.astype(jnp.int32)

    def in_group(other):
        return (gx, y_hi * group + other, gz)

    def in_line(other):
        return (other, gy, gz)

    def in_columns(other):
        return (gx, (other // nz) * group + rank, lax.rem(other, nz))

    for step in range(1, group):
        pl.semaphore_signal(
            barrier, inc=1, device_id=in_group(lax.rem(rank + step, group)), device_id_type=MESH
        )
    for step in range(1, nx):
        pl.semaphore_signal(
            barrier, inc=1, device_id=in_line(lax.rem(gx + step, nx)), device_id_type=MESH
        )
    for step in range(1, columns):
        pl.semaphore_signal(
            barrier, inc=1, device_id=in_columns(lax.rem(column + step, columns)), device_id_type=MESH
        )
    pl.semaphore_wait(barrier, expected)

    pieces = [
        ((0, 0, 1), field_ref.at[:, 7], halo.at[:, 0, 1:]),
        ((0, 1, 0), field_ref.at[:, :, 7], halo.at[:, 1:, 0]),
        ((0, 1, 1), field_ref.at[:, 7, 7], halo.at[:, 0, 0]),
    ]
    inputs = []
    for i, (up, src, dst) in enumerate(pieces):
        above, device = shifted(*up)
        below, _ = shifted(*(-v for v in up))
        copy = remote(src, dst, send_in.at[i], recv_in.at[i], device)
        inputs.append((copy, above, below))
        pl.when(above)(copy.start)

    lane = iota((128, 128), 1)
    row = iota((128, 128), 0)
    order = (lane == lax.rem(row, 2) * 64 + row // 2).astype(bf16)
    for kz in range(3):
        for block, kx in enumerate((1, 2, 0)):
            both = jnp.concatenate([w_ref[kz, 1, kx], w_ref[kz, 2, kx]], axis=0)
            only = jnp.concatenate([jnp.zeros((64, 128), bf16), w_ref[kz, 0, kx]], axis=0)
            taps[kz, 1, 128 * block : 128 * block + 128] = dot(order, both).astype(bf16)
            taps[kz, 0, 128 * block : 128 * block + 128] = dot(order, only).astype(bf16)

    sel = (lane == jnp.where(row < 64, 2 * row, 2 * row - 127)).astype(bf16)

    def place(z, y, block):
        odd = block[64:]
        rows[z, y, :, 0:128] = block[:64].astype(bf16)
        rows[z, y, :, 128:256] = odd.astype(bf16)
        rows[z, y, :, 256:384] = pltpu.roll(odd, 1, 0).astype(bf16)

    own.wait()

    @pl.loop(1, 9)
    def _(z):
        for y in range(1, 9, 2):
            tile = jnp.concatenate(
                [halo[:, z, y].reshape(128, 128), halo[:, z, y + 1].reshape(128, 128)], axis=0
            )
            both = split_rows(sel, tile)
            for side in range(2):
                block = both[:, 128 * side : 128 * side + 128]
                place(z, y + side, block)
                edge_out[z - 1, y + side - 1] = block[127:128]

    rims = [
        ((1, 0, 0), edge_out, edge_in.at[1:, 1:]),
        ((1, 0, 1), edge_out.at[7], edge_in.at[0, 1:]),
        ((1, 1, 0), edge_out.at[:, 7], edge_in.at[1:, 0]),
        ((1, 1, 1), edge_out.at[7, 7], edge_in.at[0, 0]),
    ]
    for i, (up, src, dst) in enumerate(rims):
        above, device = shifted(*up)
        below, _ = shifted(*(-v for v in up))
        copy = remote(src, dst, send_in.at[3 + i], recv_in.at[3 + i], device)
        inputs.append((copy, above, below))
        pl.when(above)(copy.start)

    def patch(z):
        first = rows[z, :, 0:16, 256:384].astype(f32)
        rim = jnp.broadcast_to(edge_in[z], (9, 16, 128))
        rows[z, :, 0:16, 256:384] = jnp.where(iota((9, 16, 128), 1) == 0, rim, first).astype(bf16)

    def conv_plane(zo):
        for part_y in range(2):
            total = None
            for kz in range(3):
                for j in range(2):
                    lhs = rows[2 * zo + kz, pl.ds(4 * part_y + j, 4)].reshape(256, 384)
                    term = dot(lhs, taps[kz, j])
                    total = term if total is None else total + term
            feat_ref[zo + 1, 1 + 4 * part_y : 5 + 4 * part_y] = total.reshape(4, 64, 128)
            if part_y == 0:
                summed = jnp.sum(total, axis=0, keepdims=True)
            else:
                summed = summed + jnp.sum(total, axis=0, keepdims=True)
        return summed

    for i in (1, 3, 5):
        copy, _, below = inputs[i]
        pl.when(below)(copy.wait_recv)
    has_y = gy > 0
    has_z = gz > 0

    @pl.when(has_y)
    def _():
        @pl.loop(1, 9)
        def _(z):
            place(z, 0, split_rows(sel, halo[:, z, 0].reshape(128, 128)))

    @pl.when(jnp.logical_not(has_y))
    def _():
        rows[:, 0] = jnp.zeros((9, 64, 384), bf16)

    @pl.loop(1, 9)
    def _(z):
        patch(z)

    channel_sum = lax.fori_loop(
        1, 4, lambda zo, s: s + conv_plane(zo), jnp.zeros((1, 128), f32)
    )

    for i in (0, 2, 4, 6):
        copy, _, below = inputs[i]
        pl.when(below)(copy.wait_recv)

    @pl.when(has_z)
    def _():
        @pl.loop(1, 9)
        def _(y):
            place(0, y, split_rows(sel, halo[:, 0, y].reshape(128, 128)))

    @pl.when(jnp.logical_not(has_z))
    def _():
        rows[0] = jnp.zeros((9, 64, 384), bf16)

    @pl.when(jnp.logical_and(has_z, has_y))
    def _():
        place(0, 0, split_rows(sel, halo[:, 0, 0].reshape(128, 128)))

    @pl.when(jnp.logical_and(has_z, jnp.logical_not(has_y)))
    def _():
        rows[0, 0] = jnp.zeros((64, 384), bf16)

    patch(0)
    channel_sum = channel_sum + conv_plane(0)

    cells = 4 * 8 * 64
    mean = channel_sum / cells

    def moments(z, total):
        centred = feat_ref[z, 1:9].reshape(512, 128) - mean
        return total + dot_tn(centred, centred, HIGHEST)

    square = lax.fori_loop(1, 5, moments, jnp.zeros((128, 128), f32))
    share = 64 // group
    part[:, 0:share] = diagonal_blocks(square).reshape(group, share, 128)
    part[:, share : share + 8] = jnp.broadcast_to(mean, (group, 8, 128))

    def exchange(index, members, me, device_of, source, keep):
        slots = stage.at[index]
        slots[me] = keep
        copies = []
        for step in range(1, members):
            other = lax.rem(me + step, members)
            copy = remote(
                source(other),
                slots.at[me],
                send_ar.at[index, other],
                recv_ar.at[index, me],
                device_of(other),
            )
            copy.start()
            copies.append(copy)
        return copies

    def settle(index, members, me, device_of, source):
        slots = stage.at[index]
        for step in range(1, members):
            other = lax.rem(me + step, members)
            remote(
                source(other),
                slots.at[other],
                send_ar.at[index, other],
                recv_ar.at[index, other],
                device_of(other),
            ).wait_recv()

    def merge(index, members, count):
        slots = stage.at[index]
        means = jnp.concatenate([slots[k, share : share + 1] for k in range(members)], axis=0)
        centre = jnp.sum(means, axis=0, keepdims=True) / members
        apart = means - centre
        if members < 8:
            apart = jnp.concatenate([apart, jnp.zeros((8 - members, 128), f32)], axis=0)
        outer[...] = diagonal_blocks(dot_tn(apart, apart, HIGHEST))
        between = outer[pl.ds(pl.multiple_of(rank * share, share), share)]
        total = slots[0, 0:share]
        for k in range(1, members):
            total = total + slots[k, 0:share]
        total = total + count * between
        return jnp.concatenate([total, jnp.broadcast_to(centre, (8, 128))], axis=0), centre

    first = lambda other: part.at[other]
    copies = exchange(0, group, rank, in_group, first, part[rank])

    outputs = []

    def send(index, towards, src, dst):
        there, device = shifted(*towards)
        back, _ = shifted(*(-v for v in towards))
        copy = remote(src, dst, send_out.at[index], recv_out.at[index], device)
        outputs.append((copy, there, back))
        pl.when(there)(copy.start)

    def await_in(indices):
        for i in indices:
            copy, _, back = outputs[i]
            pl.when(back)(copy.wait_recv)

    low = feat_ref[1:5, 1:9, 0:1]
    high = feat_ref[1:5, 1:9, 63:64]
    mine[0] = low
    mine[1] = high
    send(0, (-1, 0, 0), mine.at[0], rim_ref.at[1, 1:5, 1:9])
    send(1, (1, 0, 0), mine.at[1], rim_ref.at[0, 1:5, 1:9])
    send(2, (0, -1, 0), feat_ref.at[1:5, 1], feat_ref.at[1:5, 9])
    send(3, (0, 1, 0), feat_ref.at[1:5, 8], feat_ref.at[1:5, 0])
    send(4, (0, 0, -1), feat_ref.at[1, 1:9], feat_ref.at[5, 1:9])
    send(5, (0, 0, 1), feat_ref.at[4, 1:9], feat_ref.at[0, 1:9])

    settle(0, group, rank, in_group, first)
    merged, _ = merge(0, group, float(cells))
    await_in((0, 1))
    send(6, (0, -1, 0), rim_ref.at[:, 1:5, 1], rim_ref.at[:, 1:5, 9])
    send(7, (0, 1, 0), rim_ref.at[:, 1:5, 8], rim_ref.at[:, 1:5, 0])

    second = lambda other: stage.at[1, gx]
    copies += exchange(1, nx, gx, in_line, second, merged)
    settle(1, nx, gx, in_line, second)
    merged, _ = merge(1, nx, float(cells * group))

    third = lambda other: stage.at[2, column]
    copies += exchange(2, columns, column, in_columns, third, merged)

    await_in((2, 3, 6, 7))
    send(8, (0, 0, -1), feat_ref.at[1, 0], feat_ref.at[5, 0])
    send(9, (0, 0, -1), feat_ref.at[1, 9], feat_ref.at[5, 9])
    send(10, (0, 0, 1), feat_ref.at[4, 0], feat_ref.at[0, 0])
    send(11, (0, 0, 1), feat_ref.at[4, 9], feat_ref.at[0, 9])
    send(12, (0, 0, -1), rim_ref.at[:, 1], rim_ref.at[:, 5])
    send(13, (0, 0, 1), rim_ref.at[:, 4], rim_ref.at[:, 0])

    settle(2, columns, column, in_columns, third)
    merged, centre = merge(2, columns, float(cells * group * nx))

    fourth = lambda other: stage.at[3, rank]
    copies += exchange(3, group, rank, in_group, fourth, merged)
    settle(3, group, rank, in_group, fourth)
    mom_ref[...] = stage[3, 0:group, 0:share].reshape(64, 128)
    mean_ref[...] = centre

    await_in((4, 5, 8, 9, 10, 11, 12, 13))
    for copy in copies:
        copy.wait_send()
    for copy, there, _ in inputs + outputs:
        pl.when(there)(copy.wait_send)


def result_kernel(
    sizes, feat_ref, rim_ref, mom_ref, mean_ref, gain_ref, shift_ref, w_ref, out_ref, acts
):
    nx, ny, nz = sizes
    gx, gy, gz = (lax.axis_index(a) for a in AXES)
    cells = 4 * 8 * 64 * nx * ny * nz
    mean = mean_ref[...]
    lane = iota((128, 128), 1)
    row = iota((128, 128), 0)
    half = (lane < 64) == (row < 64)
    eye = (lane == row).astype(f32)
    tiled = jnp.concatenate([mom_ref[...], mom_ref[...]], axis=0)
    covariance = jnp.where(half, tiled / cells, 0.0) + EPSILON * eye
    diagonal = jnp.sum(covariance * eye, axis=0, keepdims=True)
    head = iota((1, 128), 1) < 64
    trace_0 = jnp.sum(jnp.where(head, diagonal, 0.0), axis=1, keepdims=True)
    trace_1 = jnp.sum(jnp.where(head, 0.0, diagonal), axis=1, keepdims=True)
    trace = jnp.where(head, trace_0, trace_1)
    scaled = covariance / trace
    newton = 1.5 * eye - 0.5 * scaled
    for _ in range(NEWTON - 1):
        square = dot(newton, newton, HIGHEST)
        times = dot(newton, scaled, HIGHEST)
        newton = 1.5 * newton - 0.5 * dot(square, times, HIGHEST)
    whitener = newton / jnp.sqrt(trace)
    mixing = dot_nt(eye, whitener, HIGHEST) * gain_ref[...]
    mix_hi = mixing.astype(bf16)
    mix_lo = (mixing - mix_hi.astype(f32)).astype(bf16)
    top = jnp.concatenate([mix_hi, mix_lo], axis=1)
    bottom = jnp.concatenate([mix_hi, jnp.zeros((128, 128), bf16)], axis=1)
    mixer = jnp.concatenate([top, bottom], axis=0)

    def activate(block):
        centred = block - mean
        hi = centred.astype(bf16)
        lo = (centred - hi.astype(f32)).astype(bf16)
        both = dot(jnp.concatenate([hi, lo], axis=1), mixer)
        value = both[:, :128] + both[:, 128:] + shift_ref[...]
        return jnp.where(value >= 0, value, LEAK * value)

    in_z = (gz > 0, gz < nz - 1)
    in_y = (gy > 0, gy < ny - 1)
    in_x = (gx > 0, gx < nx - 1)

    @pl.loop(0, 6)
    def _(z):
        keep_z = jnp.logical_and(
            jnp.logical_or(z > 0, in_z[0]), jnp.logical_or(z < 5, in_z[1])
        )
        y = iota((10, 64, 128), 0)
        keep = jnp.logical_and(
            jnp.logical_and(jnp.logical_or(y > 0, in_y[0]), jnp.logical_or(y < 9, in_y[1])), keep_z
        )
        act = activate(feat_ref[z].reshape(640, 128))
        act = jnp.where(keep, act.reshape(10, 64, 128), 0.0)
        x = iota((10, 64, 128), 1)
        flat = act.reshape(640, 128)
        moved = []
        for side in range(2):
            rim = rim_ref[side, z].reshape(10, 128)
            rim = jnp.concatenate([rim, jnp.zeros((6, 128), f32)], axis=0)
            rim = activate(rim)[0:10].reshape(10, 1, 128)
            rim = jnp.where(jnp.logical_and(keep[:, 0:1], in_x[side]), rim, 0.0)
            turned = pltpu.roll(flat, 1 if side == 0 else 639, 0).reshape(10, 64, 128)
            moved.append(
                jnp.where(x == (0 if side == 0 else 63), jnp.broadcast_to(rim, (10, 64, 128)), turned)
            )
        acts[z, :, :, 0:128] = moved[0].astype(bf16)
        acts[z, :, :, 128:256] = act.astype(bf16)
        acts[z, :, :, 256:384] = moved[1].astype(bf16)

    @pl.loop(0, 4)
    def _(z):
        for part_y in range(2):
            total = None
            for kz in range(3):
                for ky in range(3):
                    lhs = acts[z + kz, pl.ds(4 * part_y + ky, 4)].reshape(256, 384)
                    term = dot(lhs, w_ref[3 * kz + ky])
                    total = term if total is None else total + term
            out_ref[z, 256 * part_y : 256 * part_y + 256] = total.astype(bf16)


VMEM = pl.BlockSpec(memory_space=pltpu.VMEM)


def body(sizes, field, conv_first, norm_gain, norm_shift, conv_second):
    nx, ny, nz = sizes
    group = ny // 2
    share = 64 // group
    slots = max(group, nx, 2 * nz)
    dma = pltpu.SemaphoreType.DMA
    feat, rim, mom, mean = pl.pallas_call(
        functools.partial(features_kernel, sizes),
        name="features",
        out_shape=(
            jax.ShapeDtypeStruct((6, 10, 64, 128), f32),
            jax.ShapeDtypeStruct((2, 6, 10, 1, 128), f32),
            jax.ShapeDtypeStruct((64, 128), f32),
            jax.ShapeDtypeStruct((1, 128), f32),
        ),
        in_specs=[pl.BlockSpec(memory_space=pl.ANY), VMEM],
        out_specs=(VMEM, VMEM, VMEM, VMEM),
        scratch_shapes=[
            pltpu.VMEM((64, 9, 9, 2, 128), bf16),
            pltpu.VMEM((9, 9, 64, 384), bf16),
            pltpu.VMEM((3, 2, 384, 128), bf16),
            pltpu.VMEM((8, 8, 1, 128), f32),
            pltpu.VMEM((9, 9, 1, 128), f32),
            pltpu.VMEM((4, slots, share + 8, 128), f32),
            pltpu.VMEM((group, share + 8, 128), f32),
            pltpu.VMEM((64, 128), f32),
            pltpu.VMEM((2, 4, 8, 1, 128), f32),
            dma((8,)),
            dma((7,)),
            dma((14,)),
            dma((14,)),
            dma((4, slots)),
            dma((4, slots)),
        ],
        compiler_params=pltpu.CompilerParams(
            collective_id=0, has_side_effects=True, vmem_limit_bytes=60000 * 1024
        ),
    )(field.reshape(64, 8, 8, 2, 128), conv_first)
    cells = pl.pallas_call(
        functools.partial(result_kernel, sizes),
        name="result",
        out_shape=jax.ShapeDtypeStruct((4, 512, 128), bf16),
        in_specs=[VMEM] * 7,
        out_specs=VMEM,
        scratch_shapes=[pltpu.VMEM((6, 10, 64, 384), bf16)],
        compiler_params=pltpu.CompilerParams(vmem_limit_bytes=60000 * 1024),
    )(
        feat,
        rim,
        mom,
        mean,
        norm_gain.reshape(1, 128),
        norm_shift.reshape(1, 128),
        conv_second.reshape(9, 384, 128),
    )
    return cells.reshape(2048, 128).T.reshape(128, 4, 8, 64)


def solution(mesh):
    sizes = tuple(mesh.shape[a] for a in AXES)
    in_specs = (P(None, "gz", "gy", "gx"), P(), P(), P(), P())
    out_specs = P(None, "gz", "gy", "gx")
    return jax.shard_map(
        functools.partial(body, sizes), mesh=mesh, in_specs=in_specs, out_specs=out_specs, check_vma=False
    )
```

```python
import functools

import jax
import jax.numpy as jnp
from jax import lax
from jax.experimental import pallas as pl
from jax.experimental.pallas import tpu as pltpu
from jax.sharding import PartitionSpec as P

NEWTON = 5
EPSILON = 1e-05
LEAK = 0.2
AXES = ("gx", "gy", "gz")
MESH = pl.DeviceIdType.MESH
HIGHEST = lax.Precision.HIGHEST
f32 = jnp.float32
bf16 = jnp.bfloat16


def iota(shape, dim):
    return lax.broadcasted_iota(jnp.int32, shape, dim)


def contract(a, b, dim_a, dim_b, precision=None):
    return lax.dot_general(
        a, b, (((dim_a,), (dim_b,)), ((), ())), preferred_element_type=f32, precision=precision
    )


def dot(a, b, precision=None):
    return contract(a, b, 1, 0, precision)


def dot_nt(a, b, precision=None):
    return contract(a, b, 1, 1, precision)


def dot_tn(a, b, precision=None):
    return contract(a, b, 0, 0, precision)


def halves(value):
    high = value.astype(bf16)
    return high, (value - high.astype(f32)).astype(bf16)


def diagonal_blocks(square):
    half = square.shape[0] // 2
    lane = iota((half, 2 * half), 1)
    return jnp.where(lane < half, square[:half], square[half:])


def kernel(
    sizes,
    field_ref,
    first_ref,
    gain_ref,
    shift_ref,
    second_ref,
    out_ref,
    halo,
    rows,
    first,
    taps,
    second,
    edge_out,
    edge_in,
    face_out,
    face_in,
    feat,
    rim,
    mine,
    acts,
    part,
    stage,
    means,
    outer,
    send_in,
    recv_in,
    send_out,
    recv_out,
    send_ar,
    recv_ar,
    send_mean,
    recv_mean,
    local,
):
    nx, ny, nz = sizes
    gx, gy, gz = (lax.axis_index(a) for a in AXES)
    group = ny // 2
    share = 64 // group
    rank = lax.rem(gy, group)
    y_hi = gy // group
    column = y_hi * nz + gz
    columns = 2 * nz

    def shifted(dx, dy, dz):
        ok = []
        if dx:
            ok.append(gx < nx - 1 if dx > 0 else gx > 0)
        if dy:
            ok.append(gy < ny - 1 if dy > 0 else gy > 0)
        if dz:
            ok.append(gz < nz - 1 if dz > 0 else gz > 0)
        return functools.reduce(jnp.logical_and, ok), (
            jnp.clip(gx + dx, 0, nx - 1),
            jnp.clip(gy + dy, 0, ny - 1),
            jnp.clip(gz + dz, 0, nz - 1),
        )

    def remote(src, dst, send, recv, device):
        return pltpu.make_async_remote_copy(
            src_ref=src, dst_ref=dst, send_sem=send, recv_sem=recv, device_id=device, device_id_type=MESH
        )

    def in_group(other):
        return (gx, y_hi * group + other, gz)

    def in_line(other):
        return (other, gy, gz)

    def in_columns(other):
        return (gx, (other // nz) * group + rank, lax.rem(other, nz))

    sets = [(group, rank, in_group), (nx, gx, in_line), (columns, column, in_columns)]

    edge_in[...] = jnp.zeros(edge_in.shape, f32)
    own_last = pltpu.make_async_copy(field_ref.at[:, :, 7], halo.at[:, 1:, 8], local.at[0])
    own_rest = pltpu.make_async_copy(field_ref.at[:, :, 0:7], halo.at[:, 1:, 1:8], local.at[1])
    load_first = pltpu.make_async_copy(first_ref, first, local.at[2])
    load_even = pltpu.make_async_copy(second_ref, second.at[:, 0:3, :, 0:128], local.at[3])
    load_odd = pltpu.make_async_copy(second_ref, second.at[:, 1:4, :, 128:256], local.at[4])
    own_last.start()
    own_rest.start()
    load_first.start()

    barrier = pltpu.get_barrier_semaphore()
    ups = [(1, 0, 0), (0, 1, 0), (0, 0, 1), (1, 1, 0), (1, 0, 1), (0, 1, 1), (1, 1, 1)]
    expected = jnp.int32(group - 1 + nx - 1 + columns - 1)

    def greet(device):
        pl.semaphore_signal(barrier, inc=1, device_id=device, device_id_type=MESH)

    for up in ups:
        below, device = shifted(*(-v for v in up))
        pl.when(below)(functools.partial(greet, device))
        expected = expected + shifted(*up)[0].astype(jnp.int32)
    for axis in range(3):
        for sign in (-1, 1):
            there, device = shifted(*(sign if a == axis else 0 for a in range(3)))
            pl.when(there)(functools.partial(greet, device))
            expected = expected + there.astype(jnp.int32)
    for members, me, device_of in sets:

        @pl.loop(1, members)
        def _(step):
            greet(device_of(lax.rem(me + step, members)))

    pl.semaphore_wait(barrier, expected)

    pieces = {
        "z": ((0, 0, 1), field_ref.at[:, 7], halo.at[:, 0, 1:]),
        "y": ((0, 1, 0), face_out, face_in.at[1:]),
        "yz": ((0, 1, 1), face_out.at[7], face_in.at[0]),
        "xy": ((1, 1, 0), edge_out.at[:, 7], edge_in.at[1:, 0]),
        "xyz": ((1, 1, 1), edge_out.at[7, 7], edge_in.at[0, 0]),
        "xz": ((1, 0, 1), edge_out.at[7], edge_in.at[0, 1:]),
        "x": ((1, 0, 0), edge_out, edge_in.at[1:, 1:]),
    }
    inputs = {}
    for i, (name, (up, src, dst)) in enumerate(pieces.items()):
        above, device = shifted(*up)
        below, _ = shifted(*(-v for v in up))
        inputs[name] = (remote(src, dst, send_in.at[i], recv_in.at[i], device), above, below)

    def start_in(*names):
        for name in names:
            pl.when(inputs[name][1])(inputs[name][0].start)

    def await_in(*names):
        for name in names:
            pl.when(inputs[name][2])(inputs[name][0].wait_recv)

    start_in("z")
    load_even.start()
    load_odd.start()

    lane = iota((128, 128), 1)
    row = iota((128, 128), 0)
    sel = (lane == jnp.where(row < 64, 2 * row, 2 * row - 127)).astype(bf16)
    wide = iota((128, 256), 1)
    tall = iota((128, 256), 0)
    spread = (lax.rem(wide, 128) == 2 * lax.rem(tall, 64) + 1) & ((wide < 128) == (tall < 64))
    spread = spread.astype(bf16)

    def place(z, y, even, odd, edge=None):
        turned = pltpu.roll(odd, 1, 0)
        if edge is not None:
            turned = jnp.where(iota((64, 128), 0) == 0, jnp.broadcast_to(edge, (64, 128)), turned)
        rows[z, y % 2, y // 2, :, 0:128] = even.astype(bf16)
        rows[z, y % 2, y // 2, :, 128:256] = odd.astype(bf16)
        rows[z, y % 2, y // 2, :, 256:384] = turned.astype(bf16)

    def split(tiles):
        both = dot_nt(sel, jnp.concatenate([t.reshape(128, 128) for t in tiles], axis=0))
        return [(both[:64, 128 * k : 128 * k + 128], both[64:, 128 * k : 128 * k + 128]) for k in range(len(tiles))]

    own_last.wait()

    @pl.loop(0, 4)
    def _(pair):
        z = 2 * pair + 1
        for k, (even, odd) in enumerate(split([halo[:, z, 8], halo[:, z + 1, 8]])):
            place(z + k, 8, even, odd)
            edge_out[z - 1 + k, 7] = odd[63:64]

    start_in("xy", "xyz")
    face_out[...] = dot_nt(rows[1:9, 0, 4, :, 0:256].reshape(512, 256), spread).astype(bf16).reshape(8, 64, 128)
    start_in("y", "yz")
    own_rest.wait()

    @pl.loop(0, 8)
    def _(step):
        z = 8 - step
        for ys in ((1, 2), (3, 4), (5, 6), (7,)):
            for y, (even, odd) in zip(ys, split([halo[:, z, y] for y in ys])):
                place(z, y, even, odd)
                edge_out[z - 1, y - 1] = odd[63:64]

        @pl.when(step == 0)
        def _():
            start_in("xz")

    start_in("x")

    load_first.wait()
    order = (lane == lax.rem(row, 2) * 64 + row // 2).astype(bf16)
    nothing = jnp.zeros((128, 128), bf16)

    @pl.loop(0, 3)
    def _(kz):
        for block, kx in enumerate((1, 2, 0)):
            both = jnp.concatenate([first[kz, 1, kx], first[kz, 2, kx]], axis=0)
            only = jnp.concatenate([jnp.zeros((64, 128), bf16), first[kz, 0, kx]], axis=0)
            both = dot(order, both).astype(bf16)
            only = dot(order, only).astype(bf16)
            for source, (left, right) in enumerate(((only, nothing), (both, only), (nothing, both))):
                at = 384 * source + 128 * block
                taps[kz, at : at + 128, 0:128] = left
                taps[kz, at : at + 128, 128:256] = right

    await_in("x")

    @pl.loop(1, 9)
    def _(z):
        for y in range(1, 9):
            old = rows[z, y % 2, y // 2, 0:16, 256:384].astype(f32)
            edge = jnp.broadcast_to(edge_in[z, y], (16, 128))
            new = jnp.where(iota((16, 128), 0) == 0, edge, old)
            rows[z, y % 2, y // 2, 0:16, 256:384] = new.astype(bf16)

    def conv_first_rows(gather):
        total = None
        for kz in range(3):
            lhs = jnp.concatenate([gather(kz, par, skip) for par, skip in ((0, 0), (1, 0), (0, 1))], axis=1)
            term = dot(lhs, taps[kz])
            total = term if total is None else total + term
        return total

    def early(zo, carry):
        total = conv_first_rows(
            lambda kz, par, skip: rows[2 * zo + kz, par, 1 + skip : 4 + skip].reshape(192, 384)
        )
        for q in range(3):
            for par in range(2):
                feat[zo + 1, 3 + 2 * q + par] = total[64 * q : 64 * q + 64, 128 * par : 128 * par + 128]
        return carry + jnp.sum(total, axis=0, keepdims=True)

    sums = lax.fori_loop(1, 4, early, jnp.zeros((1, 256), f32))
    centre = (sums[:, :128] + sums[:, 128:]) / 1152.0

    def moments(block, carry):
        square, total = carry
        apart = block - centre
        high, low = halves(apart)
        square = square + dot_tn(high, jnp.concatenate([high, low], axis=1))
        return square, total + jnp.sum(apart, axis=0, keepdims=True)

    carry = (jnp.zeros((128, 256), f32), jnp.zeros((1, 128), f32))
    carry = lax.fori_loop(2, 5, lambda z, c: moments(feat[z, 3:9].reshape(384, 128), c), carry)

    await_in("y", "xy")
    has_y = gy > 0
    has_z = gz > 0

    def place_face(z):
        pair = dot(face_in[z], spread)
        place(z, 0, pair[:, :128], pair[:, 128:], edge_in[z, 0])

    @pl.when(has_y)
    def _():
        pl.loop(1, 9)(place_face)

    @pl.when(jnp.logical_not(has_y))
    def _():
        rows[:, 0, 0] = jnp.zeros((9, 64, 384), bf16)

    total = conv_first_rows(
        lambda kz, par, skip: jnp.concatenate([rows[2 * zo + kz, par, skip] for zo in (1, 2, 3)], axis=0)
    )
    for zo in range(1, 4):
        for par in range(2):
            feat[zo + 1, 1 + par] = total[64 * zo - 64 : 64 * zo, 128 * par : 128 * par + 128]
    carry = moments(jnp.concatenate([total[:, :128], total[:, 128:]], axis=0), carry)

    await_in("z", "yz", "xz", "xyz")

    @pl.when(has_z)
    def _():
        for ys in ((1, 2), (3, 4), (5, 6), (7, 8)):
            for y, (even, odd) in zip(ys, split([halo[:, 0, y] for y in ys])):
                place(0, y, even, odd, edge_in[0, y])

        @pl.when(has_y)
        def _():
            place_face(0)

    @pl.when(jnp.logical_not(has_z))
    def _():
        rows[0] = jnp.zeros((2, 5, 64, 384), bf16)

    total = conv_first_rows(lambda kz, par, skip: rows[kz, par, skip : 4 + skip].reshape(256, 384))
    for q in range(4):
        for par in range(2):
            feat[1, 1 + 2 * q + par] = total[64 * q : 64 * q + 64, 128 * par : 128 * par + 128]
    square, apart = moments(jnp.concatenate([total[:, :128], total[:, 128:]], axis=0), carry)

    cells = 4 * 8 * 64
    square = square[:, :128] + square[:, 128:] + square[:, 128:].T
    column_0 = jnp.where(iota((8, 128), 0) == 0, jnp.broadcast_to(apart, (8, 128)), 0.0)
    square = square - dot_tn(column_0, column_0, HIGHEST) / cells
    mean = centre + apart / cells
    part[...] = diagonal_blocks(square).reshape(group, share, 128)

    def exchange(index, members, me, device_of, source):
        def one(other, slot):
            yield remote(
                source(other), stage.at[index, slot], send_ar.at[index, other], recv_ar.at[index, slot], device_of(other)
            )
            if index < 3:
                yield remote(
                    means.at[index, me],
                    means.at[index, slot],
                    send_mean.at[index, other],
                    recv_mean.at[index, slot],
                    device_of(other),
                )

        def start():
            @pl.loop(1, members)
            def _(step):
                for copy in one(lax.rem(me + step, members), me):
                    copy.start()

        def arrive():
            @pl.loop(1, members)
            def _(step):
                other = lax.rem(me + step, members)
                for copy in one(other, other):
                    copy.wait_recv()

        def left():
            @pl.loop(1, members)
            def _(step):
                for copy in one(lax.rem(me + step, members), me):
                    copy.wait_send()

        return start, arrive, left

    def merge(index, members, count):
        several = means[index].reshape(means.shape[1], 128)[:members]
        middle = jnp.sum(several, axis=0, keepdims=True) / members
        spread_out = several - middle
        if members < 8:
            spread_out = jnp.concatenate([spread_out, jnp.zeros((8 - members, 128), f32)], axis=0)
        outer[...] = diagonal_blocks(dot_tn(spread_out, spread_out, HIGHEST))
        total = count * outer[pl.ds(pl.multiple_of(rank * share, share), share)]
        for k in range(members):
            total = total + stage[index, k]
        return total, middle

    phases = [
        exchange(0, group, rank, in_group, lambda other: part.at[other]),
        exchange(1, nx, gx, in_line, lambda other: stage.at[1, gx]),
        exchange(2, columns, column, in_columns, lambda other: stage.at[2, column]),
        exchange(3, group, rank, in_group, lambda other: stage.at[3, rank]),
    ]
    stage[0, rank] = part[rank]
    means[0, rank] = mean
    phases[0][0]()

    outputs = []

    def send(towards, src, dst):
        there, device = shifted(*towards)
        back, _ = shifted(*(-v for v in towards))
        index = len(outputs)
        copy = remote(src, dst, send_out.at[index], recv_out.at[index], device)
        outputs.append((copy, there, back))
        pl.when(there)(copy.start)

    def await_out(indices):
        for i in indices:
            copy, _, back = outputs[i]
            pl.when(back)(copy.wait_recv)

    mine[0] = feat[1:5, 1:9, 0:1]
    mine[1] = feat[1:5, 1:9, 63:64]
    send((-1, 0, 0), mine.at[0], rim.at[1, 1:5, 1:9])
    send((1, 0, 0), mine.at[1], rim.at[0, 1:5, 1:9])
    send((0, -1, 0), feat.at[1:5, 1], feat.at[1:5, 9])
    send((0, 1, 0), feat.at[1:5, 8], feat.at[1:5, 0])
    send((0, 0, -1), feat.at[1, 1:9], feat.at[5, 1:9])
    send((0, 0, 1), feat.at[4, 1:9], feat.at[0, 1:9])

    for kz in range(3):
        second[kz, 3, :, 0:128] = jnp.zeros((384, 128), bf16)
        second[kz, 0, :, 128:256] = jnp.zeros((384, 128), bf16)

    phases[0][1]()
    stage[1, gx], means[1, gx] = merge(0, group, float(cells))
    phases[1][0]()
    await_out((0, 1))
    send((0, -1, 0), rim.at[:, 1:5, 1], rim.at[:, 1:5, 9])
    send((0, 1, 0), rim.at[:, 1:5, 8], rim.at[:, 1:5, 0])
    phases[1][1]()
    stage[2, column], means[2, column] = merge(1, nx, float(cells * group))
    phases[2][0]()
    await_out((2, 3, 6, 7))
    send((0, 0, -1), feat.at[1, 0], feat.at[5, 0])
    send((0, 0, -1), feat.at[1, 9], feat.at[5, 9])
    send((0, 0, 1), feat.at[4, 0], feat.at[0, 0])
    send((0, 0, 1), feat.at[4, 9], feat.at[0, 9])
    send((0, 0, -1), rim.at[:, 1], rim.at[:, 5])
    send((0, 0, 1), rim.at[:, 4], rim.at[:, 0])
    phases[2][1]()
    stage[3, rank], average = merge(2, columns, float(cells * group * nx))
    phases[3][0]()
    await_out((4, 5, 8, 9, 10, 11, 12, 13))
    load_even.wait()
    load_odd.wait()
    phases[3][1]()

    summed = stage[3, 0:group].reshape(64, 128)
    half = (lane < 64) == (row < 64)
    eye = (lane == row).astype(f32)
    tiled = jnp.concatenate([summed, summed], axis=0)
    covariance = jnp.where(half, tiled / (cells * nx * ny * nz), 0.0) + EPSILON * eye
    diagonal = jnp.sum(covariance * eye, axis=0, keepdims=True)
    head = iota((1, 128), 1) < 64
    trace_0 = jnp.sum(jnp.where(head, diagonal, 0.0), axis=1, keepdims=True)
    trace_1 = jnp.sum(jnp.where(head, 0.0, diagonal), axis=1, keepdims=True)
    trace = jnp.where(head, trace_0, trace_1)
    scaled = covariance / trace

    def newton_step(_, newton):
        both = dot(newton, jnp.concatenate([newton, scaled], axis=1), HIGHEST)
        return 1.5 * newton - 0.5 * dot(both[:, :128], both[:, 128:], HIGHEST)

    newton = lax.fori_loop(0, NEWTON - 1, newton_step, 1.5 * eye - 0.5 * scaled)
    mixing = (newton / jnp.sqrt(trace)).T * gain_ref[...]
    mix_high, mix_low = halves(mixing)
    mixer = jnp.concatenate(
        [
            jnp.concatenate([mix_high, mix_low], axis=1),
            jnp.concatenate([mix_high, jnp.zeros((128, 128), bf16)], axis=1),
        ],
        axis=0,
    )

    def activate(block):
        both = dot(jnp.concatenate(halves(block - average), axis=1), mixer)
        value = both[:, :128] + both[:, 128:] + shift_ref[...]
        return jnp.where(value >= 0, value, LEAK * value)

    inside = (gx > 0, gx < nx - 1)

    def activate_plane(z):
        act = activate(feat[z].reshape(640, 128))
        x = iota((640, 128), 0) % 64
        kept = []
        for side in range(2):
            edge = jnp.concatenate([rim[side, z].reshape(10, 128), jnp.zeros((6, 128), f32)], axis=0)
            edge = jnp.where(inside[side], activate(edge), 0.0)[0:10].reshape(10, 1, 128)
            edge = jnp.broadcast_to(edge, (10, 64, 128)).reshape(640, 128)
            turned = pltpu.roll(act, 1 if side == 0 else 639, 0)
            kept.append(jnp.where(x == (0 if side == 0 else 63), edge, turned))
        for at, value in ((0, kept[0]), (128, act), (256, kept[1])):
            value = value.astype(bf16).reshape(5, 2, 64, 128)
            for par in range(2):
                acts[z, par, :, :, at : at + 128] = value[:, par]

    @pl.loop(0, 6)
    def _(z):
        activate_plane(z)

    @pl.when(jnp.logical_not(has_z))
    def _():
        acts[0] = jnp.zeros((2, 5, 64, 384), bf16)

    @pl.when(gz == nz - 1)
    def _():
        acts[5] = jnp.zeros((2, 5, 64, 384), bf16)

    @pl.when(jnp.logical_not(has_y))
    def _():
        acts[:, 0, 0] = jnp.zeros((6, 64, 384), bf16)

    @pl.when(gy == ny - 1)
    def _():
        acts[:, 1, 4] = jnp.zeros((6, 64, 384), bf16)

    @pl.loop(0, 4)
    def _(z):
        total = None
        for kz in range(3):
            for s in range(2):
                lhs = jnp.concatenate([acts[z + kz, par, s : s + 4].reshape(256, 384) for par in range(2)], axis=1)
                term = dot(lhs, second[kz, 2 * s : 2 * s + 2].reshape(768, 256))
                total = term if total is None else total + term
        for q in range(4):
            for par in range(2):
                out_ref[z, 2 * q + par] = total[64 * q : 64 * q + 64, 128 * par : 128 * par + 128].astype(bf16)

    for _, _, left in phases:
        left()
    for copy, there, _ in list(inputs.values()) + outputs:
        pl.when(there)(copy.wait_send)


VMEM = pl.BlockSpec(memory_space=pltpu.VMEM)
ANY = pl.BlockSpec(memory_space=pl.ANY)


def body(sizes, field, conv_first, norm_gain, norm_shift, conv_second):
    nx, ny, nz = sizes
    group = ny // 2
    share = 64 // group
    slots = max(group, nx, 2 * nz)
    dma = pltpu.SemaphoreType.DMA
    vmem = pltpu.VMEM
    cells = pl.pallas_call(
        functools.partial(kernel, sizes),
        name="block",
        out_shape=jax.ShapeDtypeStruct((4, 8, 64, 128), bf16),
        in_specs=[ANY, ANY, VMEM, VMEM, ANY],
        out_specs=VMEM,
        scratch_shapes=[
            vmem((64, 9, 9, 2, 128), bf16),
            vmem((9, 2, 5, 64, 384), bf16),
            vmem((3, 3, 3, 64, 128), bf16),
            vmem((3, 1152, 256), bf16),
            vmem((3, 4, 384, 256), bf16),
            vmem((8, 8, 1, 128), f32),
            vmem((9, 9, 1, 128), f32),
            vmem((8, 64, 128), bf16),
            vmem((9, 64, 128), bf16),
            vmem((6, 10, 64, 128), f32),
            vmem((2, 6, 10, 1, 128), f32),
            vmem((2, 4, 8, 1, 128), f32),
            vmem((6, 2, 5, 64, 384), bf16),
            vmem((group, share, 128), f32),
            vmem((4, slots, share, 128), f32),
            vmem((3, slots, 1, 128), f32),
            vmem((64, 128), f32),
            dma((7,)),
            dma((7,)),
            dma((14,)),
            dma((14,)),
            dma((4, slots)),
            dma((4, slots)),
            dma((3, slots)),
            dma((3, slots)),
            dma((5,)),
        ],
        compiler_params=pltpu.CompilerParams(
            collective_id=0, has_side_effects=True, vmem_limit_bytes=60000 * 1024
        ),
    )(
        field.reshape(64, 8, 8, 2, 128),
        conv_first,
        norm_gain.reshape(1, 128),
        norm_shift.reshape(1, 128),
        conv_second.reshape(3, 3, 384, 128),
    )
    return cells.reshape(2048, 128).T.reshape(128, 4, 8, 64)


def solution(mesh):
    sizes = tuple(mesh.shape[a] for a in AXES)
    in_specs = (P(None, "gz", "gy", "gx"), P(), P(), P(), P())
    out_specs = P(None, "gz", "gy", "gx")
    return jax.shard_map(
        functools.partial(body, sizes), mesh=mesh, in_specs=in_specs, out_specs=out_specs, check_vma=False
    )
```

```python
import functools

import jax
import jax.numpy as jnp
from jax import lax
from jax.experimental import pallas as pl
from jax.experimental.pallas import tpu as pltpu
from jax.sharding import PartitionSpec as P

NEWTON = 5
EPSILON = 1e-05
LEAK = 0.2
AXES = ("gx", "gy", "gz")
MESH = pl.DeviceIdType.MESH
HIGHEST = lax.Precision.HIGHEST
f32 = jnp.float32
bf16 = jnp.bfloat16


def iota(shape, dim):
    return lax.broadcasted_iota(jnp.int32, shape, dim)


def contract(a, b, dim_a, dim_b, precision=None):
    return lax.dot_general(
        a, b, (((dim_a,), (dim_b,)), ((), ())), preferred_element_type=f32, precision=precision
    )


def dot(a, b, precision=None):
    return contract(a, b, 1, 0, precision)


def dot_nt(a, b, precision=None):
    return contract(a, b, 1, 1, precision)


def dot_tn(a, b, precision=None):
    return contract(a, b, 0, 0, precision)


def halves(value):
    high = value.astype(bf16)
    return high, (value - high.astype(f32)).astype(bf16)


def diagonal_blocks(square):
    half = square.shape[0] // 2
    lane = iota((half, 2 * half), 1)
    return jnp.where(lane < half, square[:half], square[half:])


def kernel(
    sizes,
    field_ref,
    first_ref,
    gain_ref,
    shift_ref,
    second_ref,
    out_ref,
    halo,
    rows,
    first,
    taps,
    second,
    edge_out,
    edge_in,
    face_out,
    face_in,
    feat,
    rim,
    mine,
    acts,
    part,
    stage,
    means,
    outer,
    send_in,
    recv_in,
    send_out,
    recv_out,
    send_ar,
    recv_ar,
    send_mean,
    recv_mean,
    local,
):
    nx, ny, nz = sizes
    gx, gy, gz = (lax.axis_index(a) for a in AXES)
    group = ny // 2
    share = 64 // group
    rank = lax.rem(gy, group)
    y_hi = gy // group
    column = y_hi * nz + gz
    columns = 2 * nz

    def shifted(dx, dy, dz):
        ok = []
        if dx:
            ok.append(gx < nx - 1 if dx > 0 else gx > 0)
        if dy:
            ok.append(gy < ny - 1 if dy > 0 else gy > 0)
        if dz:
            ok.append(gz < nz - 1 if dz > 0 else gz > 0)
        return functools.reduce(jnp.logical_and, ok), (
            jnp.clip(gx + dx, 0, nx - 1),
            jnp.clip(gy + dy, 0, ny - 1),
            jnp.clip(gz + dz, 0, nz - 1),
        )

    def remote(src, dst, send, recv, device):
        return pltpu.make_async_remote_copy(
            src_ref=src, dst_ref=dst, send_sem=send, recv_sem=recv, device_id=device, device_id_type=MESH
        )

    def in_group(other):
        return (gx, y_hi * group + other, gz)

    def in_line(other):
        return (other, gy, gz)

    def in_columns(other):
        return (gx, (other // nz) * group + rank, lax.rem(other, nz))

    sets = [(group, rank, in_group), (nx, gx, in_line), (columns, column, in_columns)]

    edge_in[...] = jnp.zeros(edge_in.shape, f32)
    own_last = pltpu.make_async_copy(field_ref.at[:, :, 7], halo.at[:, 1:, 8], local.at[0])
    own_rest = pltpu.make_async_copy(field_ref.at[:, :, 0:7], halo.at[:, 1:, 1:8], local.at[1])
    load_first = pltpu.make_async_copy(first_ref, first, local.at[2])
    load_even = pltpu.make_async_copy(second_ref, second.at[:, 0:3, :, 0:128], local.at[3])
    load_odd = pltpu.make_async_copy(second_ref, second.at[:, 1:4, :, 128:256], local.at[4])
    own_last.start()
    own_rest.start()
    load_first.start()

    barrier = pltpu.get_barrier_semaphore()
    ups = [(1, 0, 0), (0, 1, 0), (0, 0, 1), (1, 1, 0), (1, 0, 1), (0, 1, 1), (1, 1, 1)]
    expected = jnp.int32(group - 1 + nx - 1 + columns - 1)

    def greet(device):
        pl.semaphore_signal(barrier, inc=1, device_id=device, device_id_type=MESH)

    for up in ups:
        below, device = shifted(*(-v for v in up))
        pl.when(below)(functools.partial(greet, device))
        expected = expected + shifted(*up)[0].astype(jnp.int32)
    for axis in range(3):
        for sign in (-1, 1):
            there, device = shifted(*(sign if a == axis else 0 for a in range(3)))
            pl.when(there)(functools.partial(greet, device))
            expected = expected + there.astype(jnp.int32)
    for members, me, device_of in sets:

        @pl.loop(1, members)
        def _(step):
            greet(device_of(lax.rem(me + step, members)))

    lane = iota((128, 128), 1)
    row = iota((128, 128), 0)
    sel = (lane == jnp.where(row < 64, 2 * row, 2 * row - 127)).astype(bf16)
    wide = iota((128, 256), 1)
    tall = iota((128, 256), 0)
    spread = (lax.rem(wide, 128) == 2 * lax.rem(tall, 64) + 1) & ((wide < 128) == (tall < 64))
    spread = spread.astype(bf16)

    def place(z, y, even, odd, edge=None):
        turned = pltpu.roll(odd, 1, 0)
        if edge is not None:
            turned = jnp.where(iota((64, 128), 0) == 0, jnp.broadcast_to(edge, (64, 128)), turned)
        rows[z, y % 2, y // 2, :, 0:128] = even.astype(bf16)
        rows[z, y % 2, y // 2, :, 128:256] = odd.astype(bf16)
        rows[z, y % 2, y // 2, :, 256:384] = turned.astype(bf16)

    def split(tiles):
        both = dot_nt(sel, jnp.concatenate([t.reshape(128, 128) for t in tiles], axis=0))
        return [(both[:64, 128 * k : 128 * k + 128], both[64:, 128 * k : 128 * k + 128]) for k in range(len(tiles))]

    own_last.wait()

    @pl.loop(0, 4)
    def _(pair):
        z = 2 * pair + 1
        for k, (even, odd) in enumerate(split([halo[:, z, 8], halo[:, z + 1, 8]])):
            place(z + k, 8, even, odd)
            edge_out[z - 1 + k, 7] = odd[63:64]

    face_out[...] = dot_nt(rows[1:9, 0, 4, :, 0:256].reshape(512, 256), spread).astype(bf16).reshape(8, 64, 128)

    pl.semaphore_wait(barrier, expected)

    pieces = {
        "z": ((0, 0, 1), field_ref.at[:, 7], halo.at[:, 0, 1:]),
        "y": ((0, 1, 0), face_out, face_in.at[1:]),
        "yz": ((0, 1, 1), face_out.at[7], face_in.at[0]),
        "xy": ((1, 1, 0), edge_out.at[:, 7], edge_in.at[1:, 0]),
        "xyz": ((1, 1, 1), edge_out.at[7, 7], edge_in.at[0, 0]),
        "xz": ((1, 0, 1), edge_out.at[7], edge_in.at[0, 1:]),
        "x": ((1, 0, 0), edge_out, edge_in.at[1:, 1:]),
    }
    inputs = {}
    for i, (name, (up, src, dst)) in enumerate(pieces.items()):
        above, device = shifted(*up)
        below, _ = shifted(*(-v for v in up))
        inputs[name] = (remote(src, dst, send_in.at[i], recv_in.at[i], device), above, below)

    def start_in(*names):
        for name in names:
            pl.when(inputs[name][1])(inputs[name][0].start)

    def await_in(*names):
        for name in names:
            pl.when(inputs[name][2])(inputs[name][0].wait_recv)

    start_in("y", "z", "xyz", "yz", "xy")
    load_even.start()
    load_odd.start()
    own_rest.wait()

    @pl.loop(0, 8)
    def _(step):
        z = 8 - step
        for ys in ((1, 2), (3, 4), (5, 6), (7,)):
            for y, (even, odd) in zip(ys, split([halo[:, z, y] for y in ys])):
                place(z, y, even, odd)
                edge_out[z - 1, y - 1] = odd[63:64]

        @pl.when(step == 0)
        def _():
            start_in("xz")

    start_in("x")

    load_first.wait()
    order = (lane == lax.rem(row, 2) * 64 + row // 2).astype(bf16)
    nothing = jnp.zeros((128, 128), bf16)

    @pl.loop(0, 3)
    def _(kz):
        for block, kx in enumerate((1, 2, 0)):
            both = jnp.concatenate([first[kz, 1, kx], first[kz, 2, kx]], axis=0)
            only = jnp.concatenate([jnp.zeros((64, 128), bf16), first[kz, 0, kx]], axis=0)
            both = dot(order, both).astype(bf16)
            only = dot(order, only).astype(bf16)
            for source, (left, right) in enumerate(((only, nothing), (both, only), (nothing, both))):
                at = 384 * source + 128 * block
                taps[kz, at : at + 128, 0:128] = left
                taps[kz, at : at + 128, 128:256] = right

    await_in("x")

    @pl.loop(1, 9)
    def _(z):
        for y in range(1, 9):
            old = rows[z, y % 2, y // 2, 0:16, 256:384].astype(f32)
            edge = jnp.broadcast_to(edge_in[z, y], (16, 128))
            new = jnp.where(iota((16, 128), 0) == 0, edge, old)
            rows[z, y % 2, y // 2, 0:16, 256:384] = new.astype(bf16)

    def conv_first_rows(gather):
        total = None
        for kz in range(3):
            lhs = jnp.concatenate([gather(kz, par, skip) for par, skip in ((0, 0), (1, 0), (0, 1))], axis=1)
            term = dot(lhs, taps[kz])
            total = term if total is None else total + term
        return total

    def early(zo, carry):
        total = conv_first_rows(
            lambda kz, par, skip: rows[2 * zo + kz, par, 1 + skip : 4 + skip].reshape(192, 384)
        )
        for q in range(3):
            for par in range(2):
                feat[zo + 1, 3 + 2 * q + par] = total[64 * q : 64 * q + 64, 128 * par : 128 * par + 128]
        return carry + jnp.sum(total, axis=0, keepdims=True)

    sums = lax.fori_loop(1, 4, early, jnp.zeros((1, 256), f32))
    centre = (sums[:, :128] + sums[:, 128:]) / 1152.0

    def moments(block, carry):
        square, total = carry
        apart = block - centre
        high, low = halves(apart)
        square = square + dot_tn(high, jnp.concatenate([high, low], axis=1))
        return square, total + jnp.sum(apart, axis=0, keepdims=True)

    carry = (jnp.zeros((128, 256), f32), jnp.zeros((1, 128), f32))
    carry = lax.fori_loop(2, 5, lambda z, c: moments(feat[z, 3:9].reshape(384, 128), c), carry)

    await_in("y", "xy")
    has_y = gy > 0
    has_z = gz > 0

    def place_face(z):
        pair = dot(face_in[z], spread)
        place(z, 0, pair[:, :128], pair[:, 128:], edge_in[z, 0])

    @pl.when(has_y)
    def _():
        pl.loop(1, 9)(place_face)

    @pl.when(jnp.logical_not(has_y))
    def _():
        rows[:, 0, 0] = jnp.zeros((9, 64, 384), bf16)

    total = conv_first_rows(
        lambda kz, par, skip: jnp.concatenate([rows[2 * zo + kz, par, skip] for zo in (1, 2, 3)], axis=0)
    )
    for zo in range(1, 4):
        for par in range(2):
            feat[zo + 1, 1 + par] = total[64 * zo - 64 : 64 * zo, 128 * par : 128 * par + 128]
    carry = moments(jnp.concatenate([total[:, :128], total[:, 128:]], axis=0), carry)

    await_in("z", "yz", "xz", "xyz")

    @pl.when(has_z)
    def _():
        for ys in ((1, 2), (3, 4), (5, 6), (7, 8)):
            for y, (even, odd) in zip(ys, split([halo[:, 0, y] for y in ys])):
                place(0, y, even, odd, edge_in[0, y])

        @pl.when(has_y)
        def _():
            place_face(0)

    @pl.when(jnp.logical_not(has_z))
    def _():
        rows[0] = jnp.zeros((2, 5, 64, 384), bf16)

    total = conv_first_rows(lambda kz, par, skip: rows[kz, par, skip : 4 + skip].reshape(256, 384))
    for q in range(4):
        for par in range(2):
            feat[1, 1 + 2 * q + par] = total[64 * q : 64 * q + 64, 128 * par : 128 * par + 128]
    square, apart = moments(jnp.concatenate([total[:, :128], total[:, 128:]], axis=0), carry)

    cells = 4 * 8 * 64
    square = square[:, :128] + square[:, 128:] + square[:, 128:].T
    column_0 = jnp.where(iota((8, 128), 0) == 0, jnp.broadcast_to(apart, (8, 128)), 0.0)
    square = square - dot_tn(column_0, column_0, HIGHEST) / cells
    mean = centre + apart / cells
    part[...] = diagonal_blocks(square).reshape(group, share, 128)

    def exchange(index, members, me, device_of, source):
        def one(other, slot):
            yield remote(
                source(other), stage.at[index, slot], send_ar.at[index, other], recv_ar.at[index, slot], device_of(other)
            )
            if index < 3:
                yield remote(
                    means.at[index, me],
                    means.at[index, slot],
                    send_mean.at[index, other],
                    recv_mean.at[index, slot],
                    device_of(other),
                )

        def start():
            @pl.loop(1, members)
            def _(step):
                for copy in one(lax.rem(me + step, members), me):
                    copy.start()

        def arrive():
            @pl.loop(1, members)
            def _(step):
                other = lax.rem(me + step, members)
                for copy in one(other, other):
                    copy.wait_recv()

        def left():
            @pl.loop(1, members)
            def _(step):
                for copy in one(lax.rem(me + step, members), me):
                    copy.wait_send()

        return start, arrive, left

    def merge(index, members, count):
        several = means[index].reshape(means.shape[1], 128)[:members]
        middle = jnp.sum(several, axis=0, keepdims=True) / members
        spread_out = several - middle
        if members < 8:
            spread_out = jnp.concatenate([spread_out, jnp.zeros((8 - members, 128), f32)], axis=0)
        outer[...] = diagonal_blocks(dot_tn(spread_out, spread_out, HIGHEST))
        total = count * outer[pl.ds(pl.multiple_of(rank * share, share), share)]
        for k in range(members):
            total = total + stage[index, k]
        return total, middle

    phases = [
        exchange(0, group, rank, in_group, lambda other: part.at[other]),
        exchange(1, columns, column, in_columns, lambda other: stage.at[1, column]),
        exchange(2, nx, gx, in_line, lambda other: stage.at[2, gx]),
        exchange(3, group, rank, in_group, lambda other: stage.at[3, rank]),
    ]
    stage[0, rank] = part[rank]
    means[0, rank] = mean
    phases[0][0]()

    outputs = []

    def send(towards, src, dst):
        there, device = shifted(*towards)
        back, _ = shifted(*(-v for v in towards))
        index = len(outputs)
        copy = remote(src, dst, send_out.at[index], recv_out.at[index], device)
        outputs.append((copy, there, back))
        pl.when(there)(copy.start)

    def await_out(indices):
        for i in indices:
            copy, _, back = outputs[i]
            pl.when(back)(copy.wait_recv)

    mine[0] = feat[1:5, 1:9, 0:1]
    mine[1] = feat[1:5, 1:9, 63:64]
    send((-1, 0, 0), mine.at[0], rim.at[1, 1:5, 1:9])
    send((1, 0, 0), mine.at[1], rim.at[0, 1:5, 1:9])

    for kz in range(3):
        second[kz, 3, :, 0:128] = jnp.zeros((384, 128), bf16)
        second[kz, 0, :, 128:256] = jnp.zeros((384, 128), bf16)

    phases[0][1]()
    stage[1, column], means[1, column] = merge(0, group, float(cells))
    phases[1][0]()
    send((0, -1, 0), feat.at[1:5, 1], feat.at[1:5, 9])
    send((0, 1, 0), feat.at[1:5, 8], feat.at[1:5, 0])
    await_out((0, 1))
    send((0, -1, 0), rim.at[:, 1:5, 1], rim.at[:, 1:5, 9])
    send((0, 1, 0), rim.at[:, 1:5, 8], rim.at[:, 1:5, 0])
    phases[1][1]()
    stage[2, gx], means[2, gx] = merge(1, columns, float(cells * group))
    phases[2][0]()
    send((0, 0, -1), feat.at[1, 1:9], feat.at[5, 1:9])
    send((0, 0, 1), feat.at[4, 1:9], feat.at[0, 1:9])
    phases[2][1]()
    stage[3, rank], average = merge(2, nx, float(cells * group * columns))
    phases[3][0]()
    await_out((2, 3, 4, 5))
    send((0, 0, -1), feat.at[1, 0], feat.at[5, 0])
    send((0, 0, -1), feat.at[1, 9], feat.at[5, 9])
    send((0, 0, 1), feat.at[4, 0], feat.at[0, 0])
    send((0, 0, 1), feat.at[4, 9], feat.at[0, 9])
    send((0, 0, -1), rim.at[:, 1], rim.at[:, 5])
    send((0, 0, 1), rim.at[:, 4], rim.at[:, 0])
    phases[3][1]()
    await_out((6, 7, 8, 9, 10, 11, 12, 13))
    load_even.wait()
    load_odd.wait()

    summed = stage[3, 0:group].reshape(64, 128)
    half = (lane < 64) == (row < 64)
    eye = (lane == row).astype(f32)
    tiled = jnp.concatenate([summed, summed], axis=0)
    covariance = jnp.where(half, tiled / (cells * nx * ny * nz), 0.0) + EPSILON * eye
    diagonal = jnp.sum(covariance * eye, axis=0, keepdims=True)
    head = iota((1, 128), 1) < 64
    trace_0 = jnp.sum(jnp.where(head, diagonal, 0.0), axis=1, keepdims=True)
    trace_1 = jnp.sum(jnp.where(head, 0.0, diagonal), axis=1, keepdims=True)
    trace = jnp.where(head, trace_0, trace_1)
    scaled = covariance / trace

    def newton_step(_, newton):
        both = dot(newton, jnp.concatenate([newton, scaled], axis=1), HIGHEST)
        return 1.5 * newton - 0.5 * dot(both[:, :128], both[:, 128:], HIGHEST)

    newton = lax.fori_loop(0, NEWTON - 1, newton_step, 1.5 * eye - 0.5 * scaled)
    mixing = (newton / jnp.sqrt(trace)).T * gain_ref[...]
    mix_high, mix_low = halves(mixing)
    mixer = jnp.concatenate(
        [
            jnp.concatenate([mix_high, mix_low], axis=1),
            jnp.concatenate([mix_high, jnp.zeros((128, 128), bf16)], axis=1),
        ],
        axis=0,
    )

    def activate(block):
        both = dot(jnp.concatenate(halves(block - average), axis=1), mixer)
        value = both[:, :128] + both[:, 128:] + shift_ref[...]
        return jnp.where(value >= 0, value, LEAK * value)

    inside = (gx > 0, gx < nx - 1)
    beyond_y = ((0, has_y), (9, gy < ny - 1))
    beyond_z = {0: has_z, 5: gz < nz - 1}

    def activate_plane(z):
        act = activate(feat[z].reshape(640, 128))
        act = jnp.concatenate(
            [
                jnp.where(beyond_y[0][1], act[0:64], 0.0),
                act[64:576],
                jnp.where(beyond_y[1][1], act[576:640], 0.0),
            ],
            axis=0,
        )
        if z in beyond_z:
            act = jnp.where(beyond_z[z], act, 0.0)
        x = iota((640, 128), 0) % 64
        y = iota((16, 128), 0)
        kept = []
        for side in range(2):
            edge = jnp.concatenate([rim[side, z].reshape(10, 128), jnp.zeros((6, 128), f32)], axis=0)
            keep = inside[side]
            for at, there in beyond_y:
                keep = jnp.logical_and(keep, jnp.logical_or(y != at, there))
            if z in beyond_z:
                keep = jnp.logical_and(keep, beyond_z[z])
            edge = jnp.where(keep, activate(edge), 0.0)[0:10].reshape(10, 1, 128)
            edge = jnp.broadcast_to(edge, (10, 64, 128)).reshape(640, 128)
            turned = pltpu.roll(act, 1 if side == 0 else 639, 0)
            kept.append(jnp.where(x == (0 if side == 0 else 63), edge, turned))
        for at, value in ((0, kept[0]), (128, act), (256, kept[1])):
            value = value.astype(bf16).reshape(5, 2, 64, 128)
            for par in range(2):
                acts[z, par, :, :, at : at + 128] = value[:, par]

    def conv_second_plane(z):
        total = None
        for kz in range(3):
            for s in range(2):
                lhs = jnp.concatenate([acts[z + kz, par, s : s + 4].reshape(256, 384) for par in range(2)], axis=1)
                term = dot(lhs, second[kz, 2 * s : 2 * s + 2].reshape(768, 256))
                total = term if total is None else total + term
        for q in range(4):
            for par in range(2):
                out_ref[z, 2 * q + par] = total[64 * q : 64 * q + 64, 128 * par : 128 * par + 128].astype(bf16)

    activate_plane(0)
    activate_plane(1)
    for z in range(4):
        activate_plane(z + 2)
        conv_second_plane(z)

    for _, _, left in phases:
        left()
    for copy, there, _ in list(inputs.values()) + outputs:
        pl.when(there)(copy.wait_send)


VMEM = pl.BlockSpec(memory_space=pltpu.VMEM)
ANY = pl.BlockSpec(memory_space=pl.ANY)


def body(sizes, field, conv_first, norm_gain, norm_shift, conv_second):
    nx, ny, nz = sizes
    group = ny // 2
    share = 64 // group
    slots = max(group, nx, 2 * nz)
    dma = pltpu.SemaphoreType.DMA
    vmem = pltpu.VMEM
    cells = pl.pallas_call(
        functools.partial(kernel, sizes),
        name="block",
        out_shape=pltpu.VMEM((4, 8, 64, 128), bf16),
        in_specs=[ANY, ANY, VMEM, VMEM, ANY],
        out_specs=VMEM,
        scratch_shapes=[
            vmem((64, 9, 9, 2, 128), bf16),
            vmem((9, 2, 5, 64, 384), bf16),
            vmem((3, 3, 3, 64, 128), bf16),
            vmem((3, 1152, 256), bf16),
            vmem((3, 4, 384, 256), bf16),
            vmem((8, 8, 1, 128), f32),
            vmem((9, 9, 1, 128), f32),
            vmem((8, 64, 128), bf16),
            vmem((9, 64, 128), bf16),
            vmem((6, 10, 64, 128), f32),
            vmem((2, 6, 10, 1, 128), f32),
            vmem((2, 4, 8, 1, 128), f32),
            vmem((6, 2, 5, 64, 384), bf16),
            vmem((group, share, 128), f32),
            vmem((4, slots, share, 128), f32),
            vmem((3, slots, 1, 128), f32),
            vmem((64, 128), f32),
            dma((7,)),
            dma((7,)),
            dma((14,)),
            dma((14,)),
            dma((4, slots)),
            dma((4, slots)),
            dma((3, slots)),
            dma((3, slots)),
            dma((5,)),
        ],
        compiler_params=pltpu.CompilerParams(
            collective_id=0, has_side_effects=True, vmem_limit_bytes=60000 * 1024
        ),
    )(
        field.reshape(64, 8, 8, 2, 128),
        conv_first,
        norm_gain.reshape(1, 128),
        norm_shift.reshape(1, 128),
        conv_second.reshape(3, 3, 384, 128),
    )
    return cells.reshape(2048, 128).T.reshape(128, 4, 8, 64)


def solution(mesh):
    sizes = tuple(mesh.shape[a] for a in AXES)
    in_specs = (P(None, "gz", "gy", "gx"), P(), P(), P(), P())
    out_specs = P(None, "gz", "gy", "gx")
    return jax.shard_map(
        functools.partial(body, sizes), mesh=mesh, in_specs=in_specs, out_specs=out_specs, check_vma=False
    )
```

```python
import functools

import jax
import jax.numpy as jnp
from jax import lax
from jax.experimental import pallas as pl
from jax.experimental.pallas import tpu as pltpu
from jax.sharding import PartitionSpec as P

NEWTON = 5
EPSILON = 1e-05
LEAK = 0.2
AXES = ("gx", "gy", "gz")
MESH = pl.DeviceIdType.MESH
HIGHEST = lax.Precision.HIGHEST
f32 = jnp.float32
bf16 = jnp.bfloat16


def iota(shape, dim):
    return lax.broadcasted_iota(jnp.int32, shape, dim)


def contract(a, b, dim_a, dim_b, precision=None):
    return lax.dot_general(
        a, b, (((dim_a,), (dim_b,)), ((), ())), preferred_element_type=f32, precision=precision
    )


def dot(a, b, precision=None):
    return contract(a, b, 1, 0, precision)


def dot_nt(a, b, precision=None):
    return contract(a, b, 1, 1, precision)


def dot_tn(a, b, precision=None):
    return contract(a, b, 0, 0, precision)


def halves(value):
    high = value.astype(bf16)
    return high, (value - high.astype(f32)).astype(bf16)


def diagonal_blocks(square):
    half = square.shape[0] // 2
    lane = iota((half, 2 * half), 1)
    return jnp.where(lane < half, square[:half], square[half:])


def kernel(
    sizes,
    field_ref,
    first_ref,
    gain_ref,
    shift_ref,
    second_ref,
    out_ref,
    halo,
    rows,
    first,
    taps,
    second,
    edge_out,
    edge_in,
    face_out,
    face_in,
    feat,
    rim,
    mine,
    acts,
    part,
    stage,
    means,
    outer,
    send_in,
    recv_in,
    send_out,
    recv_out,
    send_ar,
    recv_ar,
    send_mean,
    recv_mean,
    local,
    token_1,
    token_2,
):
    nx, ny, nz = sizes
    gx, gy, gz = (lax.axis_index(a) for a in AXES)
    group = ny // 2
    share = 64 // group
    rank = lax.rem(gy, group)
    y_hi = gy // group
    column = y_hi * nz + gz
    columns = 2 * nz

    def shifted(dx, dy, dz):
        ok = []
        if dx:
            ok.append(gx < nx - 1 if dx > 0 else gx > 0)
        if dy:
            ok.append(gy < ny - 1 if dy > 0 else gy > 0)
        if dz:
            ok.append(gz < nz - 1 if dz > 0 else gz > 0)
        return functools.reduce(jnp.logical_and, ok), (
            jnp.clip(gx + dx, 0, nx - 1),
            jnp.clip(gy + dy, 0, ny - 1),
            jnp.clip(gz + dz, 0, nz - 1),
        )

    def remote(src, dst, send, recv, device):
        return pltpu.make_async_remote_copy(
            src_ref=src, dst_ref=dst, send_sem=send, recv_sem=recv, device_id=device, device_id_type=MESH
        )

    def in_group(other):
        return (gx, y_hi * group + other, gz)

    def in_line(other):
        return (other, gy, gz)

    def in_columns(other):
        return (gx, (other // nz) * group + rank, lax.rem(other, nz))

    sets = [(group, rank, in_group), (nx, gx, in_line), (columns, column, in_columns)]

    edge_in[...] = jnp.zeros(edge_in.shape, f32)
    own_last = pltpu.make_async_copy(field_ref.at[:, :, 7], halo.at[:, 1:, 8], local.at[0])
    own_rest = pltpu.make_async_copy(field_ref.at[:, :, 0:7], halo.at[:, 1:, 1:8], local.at[1])
    load_first = pltpu.make_async_copy(first_ref, first, local.at[2])
    load_even = pltpu.make_async_copy(second_ref, second.at[:, 0:3, :, 0:128], local.at[3])
    load_odd = pltpu.make_async_copy(second_ref, second.at[:, 1:4, :, 128:256], local.at[4])
    own_last.start()
    own_rest.start()
    load_first.start()

    barrier = pltpu.get_barrier_semaphore()
    ups = [(1, 0, 0), (0, 1, 0), (0, 0, 1), (1, 1, 0), (1, 0, 1), (0, 1, 1), (1, 1, 1)]
    expected = jnp.int32(6)

    def greet(device):
        pl.semaphore_signal(barrier, inc=1, device_id=device, device_id_type=MESH)

    for up in ups:
        below, device = shifted(*(-v for v in up))
        pl.when(below)(functools.partial(greet, device))
        expected = expected + shifted(*up)[0].astype(jnp.int32)
    for axis in range(3):
        for sign in (-1, 1):
            there, device = shifted(*(sign if a == axis else 0 for a in range(3)))
            pl.when(there)(functools.partial(greet, device))
            expected = expected + there.astype(jnp.int32)
    def around(members, me, device_of, distance, signal):
        for step in (distance, members - distance):
            signal(device_of(lax.rem(me + step, members)))

    for members, me, device_of in sets:
        around(members, me, device_of, 1, greet)

    def tell(token, distance):
        for index, (members, me, device_of) in enumerate(sets):
            around(
                members,
                me,
                device_of,
                distance,
                lambda device: pl.semaphore_signal(
                    token.at[index], inc=1, device_id=device, device_id_type=MESH
                ),
            )

    def hear(token):
        for index in range(3):
            pl.semaphore_wait(token.at[index], 2)

    lane = iota((128, 128), 1)
    row = iota((128, 128), 0)
    sel = (lane == jnp.where(row < 64, 2 * row, 2 * row - 127)).astype(bf16)
    wide = iota((128, 256), 1)
    tall = iota((128, 256), 0)
    spread = (lax.rem(wide, 128) == 2 * lax.rem(tall, 64) + 1) & ((wide < 128) == (tall < 64))
    spread = spread.astype(bf16)

    def place(z, y, even, odd, edge=None):
        turned = pltpu.roll(odd, 1, 0)
        if edge is not None:
            turned = jnp.where(iota((64, 128), 0) == 0, jnp.broadcast_to(edge, (64, 128)), turned)
        rows[z, y % 2, y // 2, :, 0:128] = even.astype(bf16)
        rows[z, y % 2, y // 2, :, 128:256] = odd.astype(bf16)
        rows[z, y % 2, y // 2, :, 256:384] = turned.astype(bf16)

    def split(tiles):
        both = dot_nt(sel, jnp.concatenate([t.reshape(128, 128) for t in tiles], axis=0))
        return [(both[:64, 128 * k : 128 * k + 128], both[64:, 128 * k : 128 * k + 128]) for k in range(len(tiles))]

    own_last.wait()

    @pl.loop(0, 4)
    def _(pair):
        z = 2 * pair + 1
        for k, (even, odd) in enumerate(split([halo[:, z, 8], halo[:, z + 1, 8]])):
            place(z + k, 8, even, odd)
            edge_out[z - 1 + k, 7] = odd[63:64]

    face_out[...] = dot_nt(rows[1:9, 0, 4, :, 0:256].reshape(512, 256), spread).astype(bf16).reshape(8, 64, 128)

    pl.semaphore_wait(barrier, expected)

    pieces = {
        "z": ((0, 0, 1), field_ref.at[:, 7], halo.at[:, 0, 1:]),
        "y": ((0, 1, 0), face_out, face_in.at[1:]),
        "yz": ((0, 1, 1), face_out.at[7], face_in.at[0]),
        "xy": ((1, 1, 0), edge_out.at[:, 7], edge_in.at[1:, 0]),
        "xyz": ((1, 1, 1), edge_out.at[7, 7], edge_in.at[0, 0]),
        "xz": ((1, 0, 1), edge_out.at[7], edge_in.at[0, 1:]),
        "x": ((1, 0, 0), edge_out, edge_in.at[1:, 1:]),
    }
    inputs = {}
    for i, (name, (up, src, dst)) in enumerate(pieces.items()):
        above, device = shifted(*up)
        below, _ = shifted(*(-v for v in up))
        inputs[name] = (remote(src, dst, send_in.at[i], recv_in.at[i], device), above, below)

    def start_in(*names):
        for name in names:
            pl.when(inputs[name][1])(inputs[name][0].start)

    def await_in(*names):
        for name in names:
            pl.when(inputs[name][2])(inputs[name][0].wait_recv)

    start_in("y", "z", "xyz", "yz", "xy")
    tell(token_1, 1)
    load_even.start()
    load_odd.start()
    own_rest.wait()

    @pl.loop(0, 8)
    def _(step):
        z = 8 - step
        for ys in ((1, 2), (3, 4), (5, 6), (7,)):
            for y, (even, odd) in zip(ys, split([halo[:, z, y] for y in ys])):
                place(z, y, even, odd)
                edge_out[z - 1, y - 1] = odd[63:64]

        @pl.when(step == 0)
        def _():
            start_in("xz")

    start_in("x")

    load_first.wait()
    order = (lane == lax.rem(row, 2) * 64 + row // 2).astype(bf16)
    nothing = jnp.zeros((128, 128), bf16)

    @pl.loop(0, 3)
    def _(kz):
        for block, kx in enumerate((1, 2, 0)):
            both = jnp.concatenate([first[kz, 1, kx], first[kz, 2, kx]], axis=0)
            only = jnp.concatenate([jnp.zeros((64, 128), bf16), first[kz, 0, kx]], axis=0)
            both = dot(order, both).astype(bf16)
            only = dot(order, only).astype(bf16)
            for source, (left, right) in enumerate(((only, nothing), (both, only), (nothing, both))):
                at = 384 * source + 128 * block
                taps[kz, at : at + 128, 0:128] = left
                taps[kz, at : at + 128, 128:256] = right

    await_in("x")

    @pl.loop(1, 9)
    def _(z):
        for y in range(1, 9):
            old = rows[z, y % 2, y // 2, 0:16, 256:384].astype(f32)
            edge = jnp.broadcast_to(edge_in[z, y], (16, 128))
            new = jnp.where(iota((16, 128), 0) == 0, edge, old)
            rows[z, y % 2, y // 2, 0:16, 256:384] = new.astype(bf16)

    def conv_first_rows(gather):
        total = None
        for kz in range(3):
            lhs = jnp.concatenate([gather(kz, par, skip) for par, skip in ((0, 0), (1, 0), (0, 1))], axis=1)
            term = dot(lhs, taps[kz])
            total = term if total is None else total + term
        return total

    def early(zo, carry):
        total = conv_first_rows(
            lambda kz, par, skip: rows[2 * zo + kz, par, 1 + skip : 4 + skip].reshape(192, 384)
        )
        for q in range(3):
            for par in range(2):
                feat[zo + 1, 3 + 2 * q + par] = total[64 * q : 64 * q + 64, 128 * par : 128 * par + 128]
        return carry + jnp.sum(total, axis=0, keepdims=True)

    sums = lax.fori_loop(1, 4, early, jnp.zeros((1, 256), f32))
    centre = (sums[:, :128] + sums[:, 128:]) / 1152.0

    def moments(block, carry):
        square, total = carry
        apart = block - centre
        high, low = halves(apart)
        square = square + dot_tn(high, jnp.concatenate([high, low], axis=1))
        return square, total + jnp.sum(apart, axis=0, keepdims=True)

    carry = (jnp.zeros((128, 256), f32), jnp.zeros((1, 128), f32))
    carry = lax.fori_loop(2, 5, lambda z, c: moments(feat[z, 3:9].reshape(384, 128), c), carry)

    hear(token_1)
    tell(token_2, 2)

    await_in("y", "xy")
    has_y = gy > 0
    has_z = gz > 0

    def place_face(z):
        pair = dot(face_in[z], spread)
        place(z, 0, pair[:, :128], pair[:, 128:], edge_in[z, 0])

    @pl.when(has_y)
    def _():
        pl.loop(1, 9)(place_face)

    @pl.when(jnp.logical_not(has_y))
    def _():
        rows[:, 0, 0] = jnp.zeros((9, 64, 384), bf16)

    total = conv_first_rows(
        lambda kz, par, skip: jnp.concatenate([rows[2 * zo + kz, par, skip] for zo in (1, 2, 3)], axis=0)
    )
    for zo in range(1, 4):
        for par in range(2):
            feat[zo + 1, 1 + par] = total[64 * zo - 64 : 64 * zo, 128 * par : 128 * par + 128]
    carry = moments(jnp.concatenate([total[:, :128], total[:, 128:]], axis=0), carry)

    await_in("z", "yz", "xz", "xyz")

    @pl.when(has_z)
    def _():
        for ys in ((1, 2), (3, 4), (5, 6), (7, 8)):
            for y, (even, odd) in zip(ys, split([halo[:, 0, y] for y in ys])):
                place(0, y, even, odd, edge_in[0, y])

        @pl.when(has_y)
        def _():
            place_face(0)

    @pl.when(jnp.logical_not(has_z))
    def _():
        rows[0] = jnp.zeros((2, 5, 64, 384), bf16)

    total = conv_first_rows(lambda kz, par, skip: rows[kz, par, skip : 4 + skip].reshape(256, 384))
    for q in range(4):
        for par in range(2):
            feat[1, 1 + 2 * q + par] = total[64 * q : 64 * q + 64, 128 * par : 128 * par + 128]
    square, apart = moments(jnp.concatenate([total[:, :128], total[:, 128:]], axis=0), carry)

    cells = 4 * 8 * 64
    square = square[:, :128] + square[:, 128:] + square[:, 128:].T
    column_0 = jnp.where(iota((8, 128), 0) == 0, jnp.broadcast_to(apart, (8, 128)), 0.0)
    square = square - dot_tn(column_0, column_0, HIGHEST) / cells
    mean = centre + apart / cells
    part[...] = diagonal_blocks(square).reshape(group, share, 128)

    def exchange(index, members, me, device_of, source):
        def one(other, slot):
            yield remote(
                source(other), stage.at[index, slot], send_ar.at[index, other], recv_ar.at[index, slot], device_of(other)
            )
            if index < 3:
                yield remote(
                    means.at[index, me],
                    means.at[index, slot],
                    send_mean.at[index, other],
                    recv_mean.at[index, slot],
                    device_of(other),
                )

        def start():
            @pl.loop(1, members)
            def _(step):
                for copy in one(lax.rem(me + step, members), me):
                    copy.start()

        def arrive():
            @pl.loop(1, members)
            def _(step):
                other = lax.rem(me + step, members)
                for copy in one(other, other):
                    copy.wait_recv()

        def left():
            @pl.loop(1, members)
            def _(step):
                for copy in one(lax.rem(me + step, members), me):
                    copy.wait_send()

        return start, arrive, left

    def merge(index, members, count):
        several = means[index].reshape(means.shape[1], 128)[:members]
        middle = jnp.sum(several, axis=0, keepdims=True) / members
        spread_out = several - middle
        if members < 8:
            spread_out = jnp.concatenate([spread_out, jnp.zeros((8 - members, 128), f32)], axis=0)
        outer[...] = diagonal_blocks(dot_tn(spread_out, spread_out, HIGHEST))
        total = count * outer[pl.ds(pl.multiple_of(rank * share, share), share)]
        for k in range(members):
            total = total + stage[index, k]
        return total, middle

    phases = [
        exchange(0, group, rank, in_group, lambda other: part.at[other]),
        exchange(1, columns, column, in_columns, lambda other: stage.at[1, column]),
        exchange(2, nx, gx, in_line, lambda other: stage.at[2, gx]),
        exchange(3, group, rank, in_group, lambda other: stage.at[3, rank]),
    ]
    hear(token_2)
    stage[0, rank] = part[rank]
    means[0, rank] = mean
    phases[0][0]()

    outputs = []

    def send(towards, src, dst):
        there, device = shifted(*towards)
        back, _ = shifted(*(-v for v in towards))
        index = len(outputs)
        copy = remote(src, dst, send_out.at[index], recv_out.at[index], device)
        outputs.append((copy, there, back))
        pl.when(there)(copy.start)

    def await_out(indices):
        for i in indices:
            copy, _, back = outputs[i]
            pl.when(back)(copy.wait_recv)

    mine[0] = feat[1:5, 1:9, 0:1]
    mine[1] = feat[1:5, 1:9, 63:64]
    send((-1, 0, 0), mine.at[0], rim.at[1, 1:5, 1:9])
    send((1, 0, 0), mine.at[1], rim.at[0, 1:5, 1:9])

    for kz in range(3):
        second[kz, 3, :, 0:128] = jnp.zeros((384, 128), bf16)
        second[kz, 0, :, 128:256] = jnp.zeros((384, 128), bf16)

    phases[0][1]()
    stage[1, column], means[1, column] = merge(0, group, float(cells))
    phases[1][0]()
    send((0, -1, 0), feat.at[1:5, 1], feat.at[1:5, 9])
    send((0, 1, 0), feat.at[1:5, 8], feat.at[1:5, 0])
    await_out((0, 1))
    send((0, -1, 0), rim.at[:, 1:5, 1], rim.at[:, 1:5, 9])
    send((0, 1, 0), rim.at[:, 1:5, 8], rim.at[:, 1:5, 0])
    phases[1][1]()
    stage[2, gx], means[2, gx] = merge(1, columns, float(cells * group))
    phases[2][0]()
    send((0, 0, -1), feat.at[1, 1:9], feat.at[5, 1:9])
    send((0, 0, 1), feat.at[4, 1:9], feat.at[0, 1:9])
    phases[2][1]()
    stage[3, rank], average = merge(2, nx, float(cells * group * columns))
    phases[3][0]()
    await_out((2, 3, 4, 5))
    send((0, 0, -1), feat.at[1, 0], feat.at[5, 0])
    send((0, 0, -1), feat.at[1, 9], feat.at[5, 9])
    send((0, 0, 1), feat.at[4, 0], feat.at[0, 0])
    send((0, 0, 1), feat.at[4, 9], feat.at[0, 9])
    send((0, 0, -1), rim.at[:, 1], rim.at[:, 5])
    send((0, 0, 1), rim.at[:, 4], rim.at[:, 0])
    phases[3][1]()
    await_out((6, 7, 8, 9, 10, 11, 12, 13))
    load_even.wait()
    load_odd.wait()

    summed = stage[3, 0:group].reshape(64, 128)
    half = (lane < 64) == (row < 64)
    eye = (lane == row).astype(f32)
    tiled = jnp.concatenate([summed, summed], axis=0)
    covariance = jnp.where(half, tiled / (cells * nx * ny * nz), 0.0) + EPSILON * eye
    diagonal = jnp.sum(covariance * eye, axis=0, keepdims=True)
    head = iota((1, 128), 1) < 64
    trace_0 = jnp.sum(jnp.where(head, diagonal, 0.0), axis=1, keepdims=True)
    trace_1 = jnp.sum(jnp.where(head, 0.0, diagonal), axis=1, keepdims=True)
    trace = jnp.where(head, trace_0, trace_1)
    scaled = covariance / trace

    def newton_step(_, newton):
        both = dot(newton, jnp.concatenate([newton, scaled], axis=1), HIGHEST)
        return 1.5 * newton - 0.5 * dot(both[:, :128], both[:, 128:], HIGHEST)

    newton = lax.fori_loop(0, NEWTON - 1, newton_step, 1.5 * eye - 0.5 * scaled)
    mixing = (newton / jnp.sqrt(trace)).T * gain_ref[...]
    mix_high, mix_low = halves(mixing)
    mixer = jnp.concatenate(
        [
            jnp.concatenate([mix_high, mix_low], axis=1),
            jnp.concatenate([mix_high, jnp.zeros((128, 128), bf16)], axis=1),
        ],
        axis=0,
    )

    def activate(block):
        both = dot(jnp.concatenate(halves(block - average), axis=1), mixer)
        value = both[:, :128] + both[:, 128:] + shift_ref[...]
        return jnp.where(value >= 0, value, LEAK * value)

    inside = (gx > 0, gx < nx - 1)
    beyond_y = ((0, has_y), (9, gy < ny - 1))
    beyond_z = {0: has_z, 5: gz < nz - 1}

    def activate_plane(z):
        act = activate(feat[z].reshape(640, 128))
        act = jnp.concatenate(
            [
                jnp.where(beyond_y[0][1], act[0:64], 0.0),
                act[64:576],
                jnp.where(beyond_y[1][1], act[576:640], 0.0),
            ],
            axis=0,
        )
        if z in beyond_z:
            act = jnp.where(beyond_z[z], act, 0.0)
        x = iota((640, 128), 0) % 64
        y = iota((16, 128), 0)
        kept = []
        for side in range(2):
            edge = jnp.concatenate([rim[side, z].reshape(10, 128), jnp.zeros((6, 128), f32)], axis=0)
            keep = inside[side]
            for at, there in beyond_y:
                keep = jnp.logical_and(keep, jnp.logical_or(y != at, there))
            if z in beyond_z:
                keep = jnp.logical_and(keep, beyond_z[z])
            edge = jnp.where(keep, activate(edge), 0.0)[0:10].reshape(10, 1, 128)
            edge = jnp.broadcast_to(edge, (10, 64, 128)).reshape(640, 128)
            turned = pltpu.roll(act, 1 if side == 0 else 639, 0)
            kept.append(jnp.where(x == (0 if side == 0 else 63), edge, turned))
        for at, value in ((0, kept[0]), (128, act), (256, kept[1])):
            value = value.astype(bf16).reshape(5, 2, 64, 128)
            for par in range(2):
                acts[z, par, :, :, at : at + 128] = value[:, par]

    def conv_second_plane(z):
        total = None
        for kz in range(3):
            for s in range(2):
                lhs = jnp.concatenate([acts[z + kz, par, s : s + 4].reshape(256, 384) for par in range(2)], axis=1)
                term = dot(lhs, second[kz, 2 * s : 2 * s + 2].reshape(768, 256))
                total = term if total is None else total + term
        for q in range(4):
            for par in range(2):
                out_ref[z, 2 * q + par] = total[64 * q : 64 * q + 64, 128 * par : 128 * par + 128].astype(bf16)

    activate_plane(0)
    activate_plane(1)
    for z in range(4):
        activate_plane(z + 2)
        conv_second_plane(z)

    for _, _, left in phases:
        left()
    for copy, there, _ in list(inputs.values()) + outputs:
        pl.when(there)(copy.wait_send)


VMEM = pl.BlockSpec(memory_space=pltpu.VMEM)
ANY = pl.BlockSpec(memory_space=pl.ANY)


def body(sizes, field, conv_first, norm_gain, norm_shift, conv_second):
    nx, ny, nz = sizes
    group = ny // 2
    share = 64 // group
    slots = max(group, nx, 2 * nz)
    dma = pltpu.SemaphoreType.DMA
    vmem = pltpu.VMEM
    cells = pl.pallas_call(
        functools.partial(kernel, sizes),
        name="block",
        out_shape=pltpu.VMEM((4, 8, 64, 128), bf16),
        in_specs=[ANY, ANY, VMEM, VMEM, ANY],
        out_specs=VMEM,
        scratch_shapes=[
            vmem((64, 9, 9, 2, 128), bf16),
            vmem((9, 2, 5, 64, 384), bf16),
            vmem((3, 3, 3, 64, 128), bf16),
            vmem((3, 1152, 256), bf16),
            vmem((3, 4, 384, 256), bf16),
            vmem((8, 8, 1, 128), f32),
            vmem((9, 9, 1, 128), f32),
            vmem((8, 64, 128), bf16),
            vmem((9, 64, 128), bf16),
            vmem((6, 10, 64, 128), f32),
            vmem((2, 6, 10, 1, 128), f32),
            vmem((2, 4, 8, 1, 128), f32),
            vmem((6, 2, 5, 64, 384), bf16),
            vmem((group, share, 128), f32),
            vmem((4, slots, share, 128), f32),
            vmem((3, slots, 1, 128), f32),
            vmem((64, 128), f32),
            dma((7,)),
            dma((7,)),
            dma((14,)),
            dma((14,)),
            dma((4, slots)),
            dma((4, slots)),
            dma((3, slots)),
            dma((3, slots)),
            dma((5,)),
            pltpu.SemaphoreType.REGULAR((3,)),
            pltpu.SemaphoreType.REGULAR((3,)),
        ],
        compiler_params=pltpu.CompilerParams(
            collective_id=0, has_side_effects=True, vmem_limit_bytes=60000 * 1024
        ),
    )(
        field.reshape(64, 8, 8, 2, 128),
        conv_first,
        norm_gain.reshape(1, 128),
        norm_shift.reshape(1, 128),
        conv_second.reshape(3, 3, 384, 128),
    )
    return cells.reshape(2048, 128).T.reshape(128, 4, 8, 64)


def solution(mesh):
    sizes = tuple(mesh.shape[a] for a in AXES)
    in_specs = (P(None, "gz", "gy", "gx"), P(), P(), P(), P())
    out_specs = P(None, "gz", "gy", "gx")
    return jax.shard_map(
        functools.partial(body, sizes), mesh=mesh, in_specs=in_specs, out_specs=out_specs, check_vma=False
    )
```

```python
import functools

import jax
import jax.numpy as jnp
from jax import lax
from jax.experimental import pallas as pl
from jax.experimental.pallas import tpu as pltpu
from jax.sharding import PartitionSpec as P

NEWTON = 5
EPSILON = 1e-05
LEAK = 0.2
AXES = ("gx", "gy", "gz")
MESH = pl.DeviceIdType.MESH
HIGHEST = lax.Precision.HIGHEST
f32 = jnp.float32
bf16 = jnp.bfloat16


def iota(shape, dim):
    return lax.broadcasted_iota(jnp.int32, shape, dim)


def contract(a, b, dim_a, dim_b, precision=None):
    return lax.dot_general(
        a, b, (((dim_a,), (dim_b,)), ((), ())), preferred_element_type=f32, precision=precision
    )


def dot(a, b, precision=None):
    return contract(a, b, 1, 0, precision)


def dot_nt(a, b, precision=None):
    return contract(a, b, 1, 1, precision)


def dot_tn(a, b, precision=None):
    return contract(a, b, 0, 0, precision)


def halves(value):
    high = value.astype(bf16)
    return high, (value - high.astype(f32)).astype(bf16)


def diagonal_blocks(square):
    half = square.shape[0] // 2
    lane = iota((half, 2 * half), 1)
    return jnp.where(lane < half, square[:half], square[half:])


def kernel(
    sizes,
    field_ref,
    first_ref,
    gain_ref,
    shift_ref,
    second_ref,
    out_ref,
    halo,
    rows,
    first,
    taps,
    second,
    edge_out,
    edge_in,
    face_out,
    face_in,
    feat,
    rim,
    mine,
    acts,
    part,
    stage,
    means,
    outer,
    send_in,
    recv_in,
    send_out,
    recv_out,
    send_ar,
    recv_ar,
    send_mean,
    recv_mean,
    local,
    token_1,
    token_2,
):
    nx, ny, nz = sizes
    gx, gy, gz = (lax.axis_index(a) for a in AXES)
    group = ny // 2
    share = 64 // group
    rank = lax.rem(gy, group)
    y_hi = gy // group
    column = y_hi * nz + gz
    columns = 2 * nz

    def shifted(dx, dy, dz):
        ok = []
        if dx:
            ok.append(gx < nx - 1 if dx > 0 else gx > 0)
        if dy:
            ok.append(gy < ny - 1 if dy > 0 else gy > 0)
        if dz:
            ok.append(gz < nz - 1 if dz > 0 else gz > 0)
        return functools.reduce(jnp.logical_and, ok), (
            jnp.clip(gx + dx, 0, nx - 1),
            jnp.clip(gy + dy, 0, ny - 1),
            jnp.clip(gz + dz, 0, nz - 1),
        )

    def remote(src, dst, send, recv, device):
        return pltpu.make_async_remote_copy(
            src_ref=src, dst_ref=dst, send_sem=send, recv_sem=recv, device_id=device, device_id_type=MESH
        )

    def in_group(other):
        return (gx, y_hi * group + other, gz)

    def in_line(other):
        return (other, gy, gz)

    def in_columns(other):
        return (gx, (other // nz) * group + rank, lax.rem(other, nz))

    sets = [(group, rank, in_group), (nx, gx, in_line), (columns, column, in_columns)]

    edge_in[...] = jnp.zeros(edge_in.shape, f32)
    own_last = pltpu.make_async_copy(field_ref.at[:, :, 7], halo.at[:, 1:, 8], local.at[0])
    own_rest = pltpu.make_async_copy(field_ref.at[:, :, 0:7], halo.at[:, 1:, 1:8], local.at[1])
    load_first = pltpu.make_async_copy(first_ref, first, local.at[2])
    load_even = pltpu.make_async_copy(second_ref, second.at[:, 0:3, :, 0:128], local.at[3])
    load_odd = pltpu.make_async_copy(second_ref, second.at[:, 1:4, :, 128:256], local.at[4])
    own_last.start()
    own_rest.start()
    load_first.start()

    barrier = pltpu.get_barrier_semaphore()
    ups = [(1, 0, 0), (0, 1, 0), (0, 0, 1), (1, 1, 0), (1, 0, 1), (0, 1, 1), (1, 1, 1)]
    expected = jnp.int32(6)

    def greet(device):
        pl.semaphore_signal(barrier, inc=1, device_id=device, device_id_type=MESH)

    for up in ups:
        below, device = shifted(*(-v for v in up))
        pl.when(below)(functools.partial(greet, device))
        expected = expected + shifted(*up)[0].astype(jnp.int32)
    for axis in range(3):
        for sign in (-1, 1):
            there, device = shifted(*(sign if a == axis else 0 for a in range(3)))
            pl.when(there)(functools.partial(greet, device))
            expected = expected + there.astype(jnp.int32)
    def around(members, me, device_of, distance, signal):
        for step in (distance, members - distance):
            signal(device_of(lax.rem(me + step, members)))

    for members, me, device_of in sets:
        around(members, me, device_of, 1, greet)

    def tell(token, distance):
        for index, (members, me, device_of) in enumerate(sets):
            around(
                members,
                me,
                device_of,
                distance,
                lambda device: pl.semaphore_signal(
                    token.at[index], inc=1, device_id=device, device_id_type=MESH
                ),
            )

    def hear(token):
        for index in range(3):
            pl.semaphore_wait(token.at[index], 2)

    lane = iota((128, 128), 1)
    row = iota((128, 128), 0)
    sel = (lane == jnp.where(row < 64, 2 * row, 2 * row - 127)).astype(bf16)
    wide = iota((128, 256), 1)
    tall = iota((128, 256), 0)
    spread = (lax.rem(wide, 128) == 2 * lax.rem(tall, 64) + 1) & ((wide < 128) == (tall < 64))
    spread = spread.astype(bf16)

    def place(z, y, even, odd, edge=None):
        turned = pltpu.roll(odd, 1, 0)
        if edge is not None:
            turned = jnp.where(iota((64, 128), 0) == 0, jnp.broadcast_to(edge, (64, 128)), turned)
        rows[z, y % 2, y // 2, :, 0:128] = even.astype(bf16)
        rows[z, y % 2, y // 2, :, 128:256] = odd.astype(bf16)
        rows[z, y % 2, y // 2, :, 256:384] = turned.astype(bf16)

    def split(tiles):
        both = dot_nt(sel, jnp.concatenate([t.reshape(128, 128) for t in tiles], axis=0))
        return [(both[:64, 128 * k : 128 * k + 128], both[64:, 128 * k : 128 * k + 128]) for k in range(len(tiles))]

    own_last.wait()

    @pl.loop(0, 4)
    def _(pair):
        z = 2 * pair + 1
        for k, (even, odd) in enumerate(split([halo[:, z, 8], halo[:, z + 1, 8]])):
            place(z + k, 8, even, odd)
            edge_out[z - 1 + k, 7] = odd[63:64]

    face_out[...] = dot_nt(rows[1:9, 0, 4, :, 0:256].reshape(512, 256), spread).astype(bf16).reshape(8, 64, 128)

    pl.semaphore_wait(barrier, expected)

    pieces = {
        "z": ((0, 0, 1), field_ref.at[:, 7], halo.at[:, 0, 1:]),
        "y": ((0, 1, 0), face_out, face_in.at[1:]),
        "yz": ((0, 1, 1), face_out.at[7], face_in.at[0]),
        "xy": ((1, 1, 0), edge_out.at[:, 7], edge_in.at[1:, 0]),
        "xyz": ((1, 1, 1), edge_out.at[7, 7], edge_in.at[0, 0]),
        "xz": ((1, 0, 1), edge_out.at[7], edge_in.at[0, 1:]),
        "x": ((1, 0, 0), edge_out, edge_in.at[1:, 1:]),
    }
    inputs = {}
    for i, (name, (up, src, dst)) in enumerate(pieces.items()):
        above, device = shifted(*up)
        below, _ = shifted(*(-v for v in up))
        inputs[name] = (remote(src, dst, send_in.at[i], recv_in.at[i], device), above, below)

    def start_in(*names):
        for name in names:
            pl.when(inputs[name][1])(inputs[name][0].start)

    def await_in(*names):
        for name in names:
            pl.when(inputs[name][2])(inputs[name][0].wait_recv)

    start_in("y", "z", "xyz", "yz", "xy")
    tell(token_1, 1)
    load_even.start()
    load_odd.start()
    own_rest.wait()

    @pl.loop(0, 8)
    def _(step):
        z = 8 - step
        for ys in ((1, 2), (3, 4), (5, 6), (7,)):
            for y, (even, odd) in zip(ys, split([halo[:, z, y] for y in ys])):
                place(z, y, even, odd)
                edge_out[z - 1, y - 1] = odd[63:64]

        @pl.when(step == 0)
        def _():
            start_in("xz")

    start_in("x")

    load_first.wait()
    order = (lane == lax.rem(row, 2) * 64 + row // 2).astype(bf16)
    nothing = jnp.zeros((128, 128), bf16)

    @pl.loop(0, 3)
    def _(kz):
        for block, kx in enumerate((1, 2, 0)):
            both = jnp.concatenate([first[kz, 1, kx], first[kz, 2, kx]], axis=0)
            only = jnp.concatenate([jnp.zeros((64, 128), bf16), first[kz, 0, kx]], axis=0)
            both = dot(order, both).astype(bf16)
            only = dot(order, only).astype(bf16)
            for source, (left, right) in enumerate(((only, nothing), (both, only), (nothing, both))):
                at = 384 * source + 128 * block
                taps[kz, at : at + 128, 0:128] = left
                taps[kz, at : at + 128, 128:256] = right

    await_in("x")

    @pl.loop(1, 9)
    def _(z):
        for y in range(1, 9):
            old = rows[z, y % 2, y // 2, 0:16, 256:384].astype(f32)
            edge = jnp.broadcast_to(edge_in[z, y], (16, 128))
            new = jnp.where(iota((16, 128), 0) == 0, edge, old)
            rows[z, y % 2, y // 2, 0:16, 256:384] = new.astype(bf16)

    def conv_first_rows(gather):
        total = None
        for kz in range(3):
            lhs = jnp.concatenate([gather(kz, par, skip) for par, skip in ((0, 0), (1, 0), (0, 1))], axis=1)
            term = dot(lhs, taps[kz])
            total = term if total is None else total + term
        return total

    def early(zo, carry):
        total = conv_first_rows(
            lambda kz, par, skip: rows[2 * zo + kz, par, 1 + skip : 4 + skip].reshape(192, 384)
        )
        for q in range(3):
            for par in range(2):
                feat[zo + 1, 3 + 2 * q + par] = total[64 * q : 64 * q + 64, 128 * par : 128 * par + 128]
        return carry + jnp.sum(total, axis=0, keepdims=True)

    sums = lax.fori_loop(1, 4, early, jnp.zeros((1, 256), f32))
    centre = (sums[:, :128] + sums[:, 128:]) / 1152.0

    def moments(block, carry):
        square, total = carry
        apart = block - centre
        high, low = halves(apart)
        square = square + dot_tn(high, jnp.concatenate([high, low], axis=1))
        return square, total + jnp.sum(apart, axis=0, keepdims=True)

    carry = (jnp.zeros((128, 256), f32), jnp.zeros((1, 128), f32))
    carry = lax.fori_loop(2, 5, lambda z, c: moments(feat[z, 3:9].reshape(384, 128), c), carry)

    hear(token_1)
    tell(token_2, 2)

    await_in("y", "xy")
    has_y = gy > 0
    has_z = gz > 0

    def place_face(z):
        pair = dot(face_in[z], spread)
        place(z, 0, pair[:, :128], pair[:, 128:], edge_in[z, 0])

    @pl.when(has_y)
    def _():
        pl.loop(1, 9)(place_face)

    @pl.when(jnp.logical_not(has_y))
    def _():
        rows[:, 0, 0] = jnp.zeros((9, 64, 384), bf16)

    total = conv_first_rows(
        lambda kz, par, skip: jnp.concatenate([rows[2 * zo + kz, par, skip] for zo in (1, 2, 3)], axis=0)
    )
    for zo in range(1, 4):
        for par in range(2):
            feat[zo + 1, 1 + par] = total[64 * zo - 64 : 64 * zo, 128 * par : 128 * par + 128]
    carry = moments(jnp.concatenate([total[:, :128], total[:, 128:]], axis=0), carry)

    await_in("z", "yz", "xz", "xyz")

    @pl.when(has_z)
    def _():
        for ys in ((1, 2), (3, 4), (5, 6), (7, 8)):
            for y, (even, odd) in zip(ys, split([halo[:, 0, y] for y in ys])):
                place(0, y, even, odd, edge_in[0, y])

        @pl.when(has_y)
        def _():
            place_face(0)

    @pl.when(jnp.logical_not(has_z))
    def _():
        rows[0] = jnp.zeros((2, 5, 64, 384), bf16)

    total = conv_first_rows(lambda kz, par, skip: rows[kz, par, skip : 4 + skip].reshape(256, 384))
    for q in range(4):
        for par in range(2):
            feat[1, 1 + 2 * q + par] = total[64 * q : 64 * q + 64, 128 * par : 128 * par + 128]
    square, apart = moments(jnp.concatenate([total[:, :128], total[:, 128:]], axis=0), carry)

    def exchange(index, members, me, device_of, source):
        def moment_copy(other, slot):
            return remote(
                source(other), stage.at[index, slot], send_ar.at[index, other], recv_ar.at[index, slot], device_of(other)
            )

        def mean_copy(other, slot):
            return remote(
                means.at[index, me],
                means.at[index, slot],
                send_mean.at[index, other],
                recv_mean.at[index, slot],
                device_of(other),
            )

        def start(make):
            for step in sorted(range(1, members), key=lambda k: -min(k, members - k)):
                make(lax.rem(me + step, members), me).start()

        def arrive(make):
            @pl.loop(1, members)
            def _(step):
                other = lax.rem(me + step, members)
                make(other, other).wait_recv()

        def left(make):
            @pl.loop(1, members)
            def _(step):
                make(lax.rem(me + step, members), me).wait_send()

        def middle(following):
            arrive(mean_copy)
            several = means[index].reshape(means.shape[1], 128)[:members]
            centre_all = jnp.sum(several, axis=0, keepdims=True) / members
            if following is not None:
                following(centre_all)
            apart_all = several - centre_all
            if members < 8:
                apart_all = jnp.concatenate([apart_all, jnp.zeros((8 - members, 128), f32)], axis=0)
            outer[...] = diagonal_blocks(dot_tn(apart_all, apart_all, HIGHEST))
            return centre_all

        def total(count):
            arrive(moment_copy)
            value = count * outer[pl.ds(pl.multiple_of(rank * share, share), share)]
            for k in range(members):
                value = value + stage[index, k]
            return value

        def send_mean_of(value):
            means[index, me] = value
            start(mean_copy)

        def finish():
            left(moment_copy)
            if index < 3:
                left(mean_copy)

        return {
            "mean": send_mean_of,
            "go": lambda: start(moment_copy),
            "arrive": lambda: arrive(moment_copy),
            "middle": middle,
            "total": total,
            "finish": finish,
        }

    phases = [
        exchange(0, group, rank, in_group, lambda other: part.at[other]),
        exchange(1, columns, column, in_columns, lambda other: stage.at[1, column]),
        exchange(2, nx, gx, in_line, lambda other: stage.at[2, gx]),
        exchange(3, group, rank, in_group, lambda other: stage.at[3, rank]),
    ]

    cells = 4 * 8 * 64
    hear(token_2)
    phases[0]["mean"](centre + apart / cells)
    square = square[:, :128] + square[:, 128:] + square[:, 128:].T
    column_0 = jnp.where(iota((8, 128), 0) == 0, jnp.broadcast_to(apart, (8, 128)), 0.0)
    square = square - dot_tn(column_0, column_0, HIGHEST) / cells
    part[...] = diagonal_blocks(square).reshape(group, share, 128)
    stage[0, rank] = part[rank]
    phases[0]["go"]()

    outputs = []

    def send(towards, src, dst):
        there, device = shifted(*towards)
        back, _ = shifted(*(-v for v in towards))
        index = len(outputs)
        copy = remote(src, dst, send_out.at[index], recv_out.at[index], device)
        outputs.append((copy, there, back))
        pl.when(there)(copy.start)

    def await_out(indices):
        for i in indices:
            copy, _, back = outputs[i]
            pl.when(back)(copy.wait_recv)

    mine[0] = feat[1:5, 1:9, 0:1]
    mine[1] = feat[1:5, 1:9, 63:64]
    send((-1, 0, 0), mine.at[0], rim.at[1, 1:5, 1:9])
    send((1, 0, 0), mine.at[1], rim.at[0, 1:5, 1:9])

    for kz in range(3):
        second[kz, 3, :, 0:128] = jnp.zeros((384, 128), bf16)
        second[kz, 0, :, 128:256] = jnp.zeros((384, 128), bf16)

    phases[0]["middle"](phases[1]["mean"])
    stage[1, column] = phases[0]["total"](float(cells))
    phases[1]["go"]()
    send((0, -1, 0), feat.at[1:5, 1], feat.at[1:5, 9])
    send((0, 1, 0), feat.at[1:5, 8], feat.at[1:5, 0])
    await_out((0, 1))
    send((0, -1, 0), rim.at[:, 1:5, 1], rim.at[:, 1:5, 9])
    send((0, 1, 0), rim.at[:, 1:5, 8], rim.at[:, 1:5, 0])
    phases[1]["middle"](phases[2]["mean"])
    stage[2, gx] = phases[1]["total"](float(cells * group))
    phases[2]["go"]()
    send((0, 0, -1), feat.at[1, 1:9], feat.at[5, 1:9])
    send((0, 0, 1), feat.at[4, 1:9], feat.at[0, 1:9])
    average = phases[2]["middle"](None)
    stage[3, rank] = phases[2]["total"](float(cells * group * columns))
    phases[3]["go"]()
    await_out((2, 3, 4, 5))
    send((0, 0, -1), feat.at[1, 0], feat.at[5, 0])
    send((0, 0, -1), feat.at[1, 9], feat.at[5, 9])
    send((0, 0, 1), feat.at[4, 0], feat.at[0, 0])
    send((0, 0, 1), feat.at[4, 9], feat.at[0, 9])
    send((0, 0, -1), rim.at[:, 1], rim.at[:, 5])
    send((0, 0, 1), rim.at[:, 4], rim.at[:, 0])
    phases[3]["arrive"]()
    await_out((6, 7, 8, 9, 10, 11, 12, 13))
    load_even.wait()
    load_odd.wait()

    summed = stage[3, 0:group].reshape(64, 128)
    half = (lane < 64) == (row < 64)
    eye = (lane == row).astype(f32)
    tiled = jnp.concatenate([summed, summed], axis=0)
    covariance = jnp.where(half, tiled / (cells * nx * ny * nz), 0.0) + EPSILON * eye
    diagonal = jnp.sum(covariance * eye, axis=0, keepdims=True)
    head = iota((1, 128), 1) < 64
    trace_0 = jnp.sum(jnp.where(head, diagonal, 0.0), axis=1, keepdims=True)
    trace_1 = jnp.sum(jnp.where(head, 0.0, diagonal), axis=1, keepdims=True)
    trace = jnp.where(head, trace_0, trace_1)
    scaled = covariance / trace

    def product(a, b):
        a_high, a_low = halves(a)
        b_high, b_low = halves(b)
        return dot(
            jnp.concatenate([a_high, a_low, a_high], axis=1), jnp.concatenate([b_high, b_high, b_low], axis=0)
        )

    def newton_step(_, newton):
        both = product(newton, jnp.concatenate([newton, scaled], axis=1))
        return 1.5 * newton - 0.5 * product(both[:, :128], both[:, 128:])

    newton = lax.fori_loop(0, NEWTON - 1, newton_step, 1.5 * eye - 0.5 * scaled)
    mixing = (newton / jnp.sqrt(trace)).T * gain_ref[...]
    mix_high, mix_low = halves(mixing)
    mixer = jnp.concatenate(
        [
            jnp.concatenate([mix_high, mix_low], axis=1),
            jnp.concatenate([mix_high, jnp.zeros((128, 128), bf16)], axis=1),
        ],
        axis=0,
    )

    def activate(block):
        both = dot(jnp.concatenate(halves(block - average), axis=1), mixer)
        value = both[:, :128] + both[:, 128:] + shift_ref[...]
        return jnp.where(value >= 0, value, LEAK * value)

    inside = (gx > 0, gx < nx - 1)
    beyond_y = ((0, has_y), (9, gy < ny - 1))
    beyond_z = {0: has_z, 5: gz < nz - 1}

    def activate_plane(z):
        act = activate(feat[z].reshape(640, 128))
        act = jnp.concatenate(
            [
                jnp.where(beyond_y[0][1], act[0:64], 0.0),
                act[64:576],
                jnp.where(beyond_y[1][1], act[576:640], 0.0),
            ],
            axis=0,
        )
        if z in beyond_z:
            act = jnp.where(beyond_z[z], act, 0.0)
        x = iota((640, 128), 0) % 64
        y = iota((16, 128), 0)
        kept = []
        for side in range(2):
            edge = jnp.concatenate([rim[side, z].reshape(10, 128), jnp.zeros((6, 128), f32)], axis=0)
            keep = inside[side]
            for at, there in beyond_y:
                keep = jnp.logical_and(keep, jnp.logical_or(y != at, there))
            if z in beyond_z:
                keep = jnp.logical_and(keep, beyond_z[z])
            edge = jnp.where(keep, activate(edge), 0.0)[0:10].reshape(10, 1, 128)
            edge = jnp.broadcast_to(edge, (10, 64, 128)).reshape(640, 128)
            turned = pltpu.roll(act, 1 if side == 0 else 639, 0)
            kept.append(jnp.where(x == (0 if side == 0 else 63), edge, turned))
        for at, value in ((0, kept[0]), (128, act), (256, kept[1])):
            value = value.astype(bf16).reshape(5, 2, 64, 128)
            for par in range(2):
                acts[z, par, :, :, at : at + 128] = value[:, par]

    def conv_second_plane(z):
        total = None
        for kz in range(3):
            for s in range(2):
                lhs = jnp.concatenate([acts[z + kz, par, s : s + 4].reshape(256, 384) for par in range(2)], axis=1)
                term = dot(lhs, second[kz, 2 * s : 2 * s + 2].reshape(768, 256))
                total = term if total is None else total + term
        for q in range(4):
            for par in range(2):
                out_ref[z, 2 * q + par] = total[64 * q : 64 * q + 64, 128 * par : 128 * par + 128].astype(bf16)

    activate_plane(0)
    activate_plane(1)
    for z in range(4):
        activate_plane(z + 2)
        conv_second_plane(z)

    for phase in phases:
        phase["finish"]()
    for copy, there, _ in list(inputs.values()) + outputs:
        pl.when(there)(copy.wait_send)


VMEM = pl.BlockSpec(memory_space=pltpu.VMEM)
ANY = pl.BlockSpec(memory_space=pl.ANY)


def body(sizes, field, conv_first, norm_gain, norm_shift, conv_second):
    nx, ny, nz = sizes
    group = ny // 2
    share = 64 // group
    slots = max(group, nx, 2 * nz)
    dma = pltpu.SemaphoreType.DMA
    vmem = pltpu.VMEM
    cells = pl.pallas_call(
        functools.partial(kernel, sizes),
        name="block",
        out_shape=pltpu.VMEM((4, 8, 64, 128), bf16),
        in_specs=[ANY, ANY, VMEM, VMEM, ANY],
        out_specs=VMEM,
        scratch_shapes=[
            vmem((64, 9, 9, 2, 128), bf16),
            vmem((9, 2, 5, 64, 384), bf16),
            vmem((3, 3, 3, 64, 128), bf16),
            vmem((3, 1152, 256), bf16),
            vmem((3, 4, 384, 256), bf16),
            vmem((8, 8, 1, 128), f32),
            vmem((9, 9, 1, 128), f32),
            vmem((8, 64, 128), bf16),
            vmem((9, 64, 128), bf16),
            vmem((6, 10, 64, 128), f32),
            vmem((2, 6, 10, 1, 128), f32),
            vmem((2, 4, 8, 1, 128), f32),
            vmem((6, 2, 5, 64, 384), bf16),
            vmem((group, share, 128), f32),
            vmem((4, slots, share, 128), f32),
            vmem((3, slots, 1, 128), f32),
            vmem((64, 128), f32),
            dma((7,)),
            dma((7,)),
            dma((14,)),
            dma((14,)),
            dma((4, slots)),
            dma((4, slots)),
            dma((3, slots)),
            dma((3, slots)),
            dma((5,)),
            pltpu.SemaphoreType.REGULAR((3,)),
            pltpu.SemaphoreType.REGULAR((3,)),
        ],
        compiler_params=pltpu.CompilerParams(
            collective_id=0, has_side_effects=True, vmem_limit_bytes=60000 * 1024
        ),
    )(
        field.reshape(64, 8, 8, 2, 128),
        conv_first,
        norm_gain.reshape(1, 128),
        norm_shift.reshape(1, 128),
        conv_second.reshape(3, 3, 384, 128),
    )
    return cells.reshape(2048, 128).T.reshape(128, 4, 8, 64)


def solution(mesh):
    sizes = tuple(mesh.shape[a] for a in AXES)
    in_specs = (P(None, "gz", "gy", "gx"), P(), P(), P(), P())
    out_specs = P(None, "gz", "gy", "gx")
    return jax.shard_map(
        functools.partial(body, sizes), mesh=mesh, in_specs=in_specs, out_specs=out_specs, check_vma=False
    )
```

```python
import functools

import jax
import jax.numpy as jnp
from jax import lax
from jax.experimental import pallas as pl
from jax.experimental.pallas import tpu as pltpu
from jax.sharding import PartitionSpec as P

NEWTON = 5
EPSILON = 1e-05
LEAK = 0.2
AXES = ("gx", "gy", "gz")
MESH = pl.DeviceIdType.MESH
HIGHEST = lax.Precision.HIGHEST
f32 = jnp.float32
bf16 = jnp.bfloat16


def iota(shape, dim):
    return lax.broadcasted_iota(jnp.int32, shape, dim)


def contract(a, b, dim_a, dim_b, precision=None):
    return lax.dot_general(
        a, b, (((dim_a,), (dim_b,)), ((), ())), preferred_element_type=f32, precision=precision
    )


def dot(a, b, precision=None):
    return contract(a, b, 1, 0, precision)


def dot_nt(a, b, precision=None):
    return contract(a, b, 1, 1, precision)


def dot_tn(a, b, precision=None):
    return contract(a, b, 0, 0, precision)


def halves(value):
    high = value.astype(bf16)
    return high, (value - high.astype(f32)).astype(bf16)


def diagonal_blocks(square):
    half = square.shape[0] // 2
    lane = iota((half, 2 * half), 1)
    return jnp.where(lane < half, square[:half], square[half:])


def kernel(
    sizes,
    field_ref,
    first_ref,
    gain_ref,
    shift_ref,
    second_ref,
    out_ref,
    halo,
    rows,
    first,
    taps,
    second,
    edge_out,
    edge_in,
    face_out,
    face_in,
    feat,
    rim,
    mine,
    acts,
    part,
    stage,
    means,
    outer,
    send_in,
    recv_in,
    send_out,
    recv_out,
    send_ar,
    recv_ar,
    send_mean,
    recv_mean,
    local,
    token_1,
    token_2,
):
    nx, ny, nz = sizes
    gx, gy, gz = (lax.axis_index(a) for a in AXES)
    group = ny // 2
    share = 64 // group
    rank = lax.rem(gy, group)
    y_hi = gy // group
    column = y_hi * nz + gz
    columns = 2 * nz

    def shifted(dx, dy, dz):
        ok = []
        if dx:
            ok.append(gx < nx - 1 if dx > 0 else gx > 0)
        if dy:
            ok.append(gy < ny - 1 if dy > 0 else gy > 0)
        if dz:
            ok.append(gz < nz - 1 if dz > 0 else gz > 0)
        return functools.reduce(jnp.logical_and, ok), (
            jnp.clip(gx + dx, 0, nx - 1),
            jnp.clip(gy + dy, 0, ny - 1),
            jnp.clip(gz + dz, 0, nz - 1),
        )

    def remote(src, dst, send, recv, device):
        return pltpu.make_async_remote_copy(
            src_ref=src, dst_ref=dst, send_sem=send, recv_sem=recv, device_id=device, device_id_type=MESH
        )

    def in_group(other):
        return (gx, y_hi * group + other, gz)

    def in_line(other):
        return (other, gy, gz)

    def in_columns(other):
        return (gx, (other // nz) * group + rank, lax.rem(other, nz))

    sets = [(group, rank, in_group), (nx, gx, in_line), (columns, column, in_columns)]

    edge_in[...] = jnp.zeros(edge_in.shape, f32)
    own_last = pltpu.make_async_copy(field_ref.at[:, :, 7], halo.at[:, 1:, 8], local.at[0])
    own_rest = pltpu.make_async_copy(field_ref.at[:, :, 0:7], halo.at[:, 1:, 1:8], local.at[1])
    load_first = pltpu.make_async_copy(first_ref, first, local.at[2])
    load_even = pltpu.make_async_copy(second_ref, second.at[:, 0:3, :, 0:128], local.at[3])
    load_odd = pltpu.make_async_copy(second_ref, second.at[:, 1:4, :, 128:256], local.at[4])
    own_last.start()
    own_rest.start()
    load_first.start()

    barrier = pltpu.get_barrier_semaphore()
    ups = [(1, 0, 0), (0, 1, 0), (0, 0, 1), (1, 1, 0), (1, 0, 1), (0, 1, 1), (1, 1, 1)]
    expected = jnp.int32(6)

    def greet(device):
        pl.semaphore_signal(barrier, inc=1, device_id=device, device_id_type=MESH)

    for up in ups:
        below, device = shifted(*(-v for v in up))
        pl.when(below)(functools.partial(greet, device))
        expected = expected + shifted(*up)[0].astype(jnp.int32)
    for axis in range(3):
        for sign in (-1, 1):
            there, device = shifted(*(sign if a == axis else 0 for a in range(3)))
            pl.when(there)(functools.partial(greet, device))
            expected = expected + there.astype(jnp.int32)
    def around(members, me, device_of, distance, signal):
        for step in (distance, members - distance):
            signal(device_of(lax.rem(me + step, members)))

    for members, me, device_of in sets:
        around(members, me, device_of, 1, greet)

    def tell(token, distance):
        for index, (members, me, device_of) in enumerate(sets):
            around(
                members,
                me,
                device_of,
                distance,
                lambda device: pl.semaphore_signal(
                    token.at[index], inc=1, device_id=device, device_id_type=MESH
                ),
            )

    def hear(token):
        for index in range(3):
            pl.semaphore_wait(token.at[index], 2)

    lane = iota((128, 128), 1)
    row = iota((128, 128), 0)
    sel = (lane == jnp.where(row < 64, 2 * row, 2 * row - 127)).astype(bf16)
    wide = iota((128, 256), 1)
    tall = iota((128, 256), 0)
    spread = (lax.rem(wide, 128) == 2 * lax.rem(tall, 64) + 1) & ((wide < 128) == (tall < 64))
    spread = spread.astype(bf16)

    def place(z, y, even, odd, edge=None):
        turned = pltpu.roll(odd, 1, 0)
        if edge is not None:
            turned = jnp.where(iota((64, 128), 0) == 0, jnp.broadcast_to(edge, (64, 128)), turned)
        rows[z, y % 2, y // 2, :, 0:128] = even.astype(bf16)
        rows[z, y % 2, y // 2, :, 128:256] = odd.astype(bf16)
        rows[z, y % 2, y // 2, :, 256:384] = turned.astype(bf16)

    def split(tiles):
        both = dot_nt(sel, jnp.concatenate([t.reshape(128, 128) for t in tiles], axis=0))
        return [(both[:64, 128 * k : 128 * k + 128], both[64:, 128 * k : 128 * k + 128]) for k in range(len(tiles))]

    own_last.wait()

    @pl.loop(0, 4)
    def _(pair):
        z = 2 * pair + 1
        for k, (even, odd) in enumerate(split([halo[:, z, 8], halo[:, z + 1, 8]])):
            place(z + k, 8, even, odd)
            edge_out[z - 1 + k, 7] = odd[63:64]

    face_out[...] = dot_nt(rows[1:9, 0, 4, :, 0:256].reshape(512, 256), spread).astype(bf16).reshape(8, 64, 128)

    pl.semaphore_wait(barrier, expected)

    pieces = {
        "z": ((0, 0, 1), field_ref.at[:, 7], halo.at[:, 0, 1:]),
        "y": ((0, 1, 0), face_out, face_in.at[1:]),
        "yz": ((0, 1, 1), face_out.at[7], face_in.at[0]),
        "xy": ((1, 1, 0), edge_out.at[:, 7], edge_in.at[1:, 0]),
        "xyz": ((1, 1, 1), edge_out.at[7, 7], edge_in.at[0, 0]),
        "xz": ((1, 0, 1), edge_out.at[7], edge_in.at[0, 1:]),
        "x": ((1, 0, 0), edge_out, edge_in.at[1:, 1:]),
    }
    inputs = {}
    for i, (name, (up, src, dst)) in enumerate(pieces.items()):
        above, device = shifted(*up)
        below, _ = shifted(*(-v for v in up))
        inputs[name] = (remote(src, dst, send_in.at[i], recv_in.at[i], device), above, below)

    def start_in(*names):
        for name in names:
            pl.when(inputs[name][1])(inputs[name][0].start)

    def await_in(*names):
        for name in names:
            pl.when(inputs[name][2])(inputs[name][0].wait_recv)

    start_in("xyz", "xy", "yz", "y", "z")
    tell(token_1, 1)
    load_even.start()
    load_odd.start()
    own_rest.wait()

    @pl.loop(0, 8)
    def _(step):
        z = 8 - step
        for ys in ((1, 2), (3, 4), (5, 6), (7,)):
            for y, (even, odd) in zip(ys, split([halo[:, z, y] for y in ys])):
                place(z, y, even, odd)
                edge_out[z - 1, y - 1] = odd[63:64]

        @pl.when(step == 0)
        def _():
            start_in("xz")

    start_in("x")

    load_first.wait()
    order = (lane == lax.rem(row, 2) * 64 + row // 2).astype(bf16)
    nothing = jnp.zeros((128, 128), bf16)

    @pl.loop(0, 3)
    def _(kz):
        for block, kx in enumerate((1, 2, 0)):
            both = jnp.concatenate([first[kz, 1, kx], first[kz, 2, kx]], axis=0)
            only = jnp.concatenate([jnp.zeros((64, 128), bf16), first[kz, 0, kx]], axis=0)
            both = dot(order, both).astype(bf16)
            only = dot(order, only).astype(bf16)
            for source, (left, right) in enumerate(((only, nothing), (both, only), (nothing, both))):
                at = 384 * source + 128 * block
                taps[kz, at : at + 128, 0:128] = left
                taps[kz, at : at + 128, 128:256] = right

    await_in("x")

    @pl.loop(1, 9)
    def _(z):
        for y in range(1, 9):
            old = rows[z, y % 2, y // 2, 0:16, 256:384].astype(f32)
            edge = jnp.broadcast_to(edge_in[z, y], (16, 128))
            new = jnp.where(iota((16, 128), 0) == 0, edge, old)
            rows[z, y % 2, y // 2, 0:16, 256:384] = new.astype(bf16)

    def conv_first_rows(gather):
        total = None
        for kz in range(3):
            lhs = jnp.concatenate([gather(kz, par, skip) for par, skip in ((0, 0), (1, 0), (0, 1))], axis=1)
            term = dot(lhs, taps[kz])
            total = term if total is None else total + term
        return total

    def early(zo, carry):
        total = conv_first_rows(
            lambda kz, par, skip: rows[2 * zo + kz, par, 1 + skip : 4 + skip].reshape(192, 384)
        )
        for q in range(3):
            for par in range(2):
                feat[zo + 1, 3 + 2 * q + par] = total[64 * q : 64 * q + 64, 128 * par : 128 * par + 128]
        return carry + jnp.sum(total, axis=0, keepdims=True)

    sums = lax.fori_loop(1, 4, early, jnp.zeros((1, 256), f32))
    centre = (sums[:, :128] + sums[:, 128:]) / 1152.0

    def moments(block, carry):
        square, total = carry
        apart = block - centre
        high, low = halves(apart)
        square = square + dot_tn(high, jnp.concatenate([high, low], axis=1))
        return square, total + jnp.sum(apart, axis=0, keepdims=True)

    carry = (jnp.zeros((128, 256), f32), jnp.zeros((1, 128), f32))
    carry = lax.fori_loop(2, 5, lambda z, c: moments(feat[z, 3:9].reshape(384, 128), c), carry)

    hear(token_1)
    tell(token_2, 2)

    await_in("y", "xy")
    has_y = gy > 0
    has_z = gz > 0

    def place_face(z):
        pair = dot(face_in[z], spread)
        place(z, 0, pair[:, :128], pair[:, 128:], edge_in[z, 0])

    @pl.when(has_y)
    def _():
        pl.loop(1, 9)(place_face)

    @pl.when(jnp.logical_not(has_y))
    def _():
        rows[:, 0, 0] = jnp.zeros((9, 64, 384), bf16)

    total = conv_first_rows(
        lambda kz, par, skip: jnp.concatenate([rows[2 * zo + kz, par, skip] for zo in (1, 2, 3)], axis=0)
    )
    for zo in range(1, 4):
        for par in range(2):
            feat[zo + 1, 1 + par] = total[64 * zo - 64 : 64 * zo, 128 * par : 128 * par + 128]
    carry = moments(jnp.concatenate([total[:, :128], total[:, 128:]], axis=0), carry)

    await_in("z", "yz", "xz", "xyz")

    @pl.when(has_z)
    def _():
        for ys in ((1, 2), (3, 4), (5, 6), (7, 8)):
            for y, (even, odd) in zip(ys, split([halo[:, 0, y] for y in ys])):
                place(0, y, even, odd, edge_in[0, y])

        @pl.when(has_y)
        def _():
            place_face(0)

    @pl.when(jnp.logical_not(has_z))
    def _():
        rows[0] = jnp.zeros((2, 5, 64, 384), bf16)

    total = conv_first_rows(lambda kz, par, skip: rows[kz, par, skip : 4 + skip].reshape(256, 384))
    for q in range(4):
        for par in range(2):
            feat[1, 1 + 2 * q + par] = total[64 * q : 64 * q + 64, 128 * par : 128 * par + 128]
    square, apart = moments(jnp.concatenate([total[:, :128], total[:, 128:]], axis=0), carry)

    def exchange(index, members, me, device_of, source):
        def moment_copy(other, slot):
            return remote(
                source(other), stage.at[index, slot], send_ar.at[index, other], recv_ar.at[index, slot], device_of(other)
            )

        def mean_copy(other, slot):
            return remote(
                means.at[index, me],
                means.at[index, slot],
                send_mean.at[index, other],
                recv_mean.at[index, slot],
                device_of(other),
            )

        def start(make):
            for step in sorted(range(1, members), key=lambda k: -min(k, members - k)):
                make(lax.rem(me + step, members), me).start()

        def arrive(make):
            @pl.loop(1, members)
            def _(step):
                other = lax.rem(me + step, members)
                make(other, other).wait_recv()

        def left(make):
            @pl.loop(1, members)
            def _(step):
                make(lax.rem(me + step, members), me).wait_send()

        def middle(following):
            arrive(mean_copy)
            several = means[index].reshape(means.shape[1], 128)[:members]
            centre_all = jnp.sum(several, axis=0, keepdims=True) / members
            if following is not None:
                following(centre_all)
            apart_all = several - centre_all
            if members < 8:
                apart_all = jnp.concatenate([apart_all, jnp.zeros((8 - members, 128), f32)], axis=0)
            outer[...] = diagonal_blocks(dot_tn(apart_all, apart_all, HIGHEST))
            return centre_all

        def total(count):
            arrive(moment_copy)
            value = count * outer[pl.ds(pl.multiple_of(rank * share, share), share)]
            for k in range(members):
                value = value + stage[index, k]
            return value

        def send_mean_of(value):
            means[index, me] = value
            start(mean_copy)

        def finish():
            left(moment_copy)
            if index < 3:
                left(mean_copy)

        return {
            "mean": send_mean_of,
            "go": lambda: start(moment_copy),
            "arrive": lambda: arrive(moment_copy),
            "middle": middle,
            "total": total,
            "finish": finish,
        }

    phases = [
        exchange(0, group, rank, in_group, lambda other: part.at[other]),
        exchange(1, columns, column, in_columns, lambda other: stage.at[1, column]),
        exchange(2, nx, gx, in_line, lambda other: stage.at[2, gx]),
        exchange(3, group, rank, in_group, lambda other: stage.at[3, rank]),
    ]

    cells = 4 * 8 * 64
    column_0 = jnp.where(iota((8, 128), 0) == 0, jnp.broadcast_to(apart, (8, 128)), 0.0)
    correction = dot_tn(column_0, column_0, HIGHEST) / cells
    hear(token_2)
    phases[0]["mean"](centre + apart / cells)
    square = square[:, :128] + square[:, 128:] + square[:, 128:].T
    square = square - correction
    part[...] = diagonal_blocks(square).reshape(group, share, 128)
    stage[0, rank] = part[rank]
    phases[0]["go"]()

    outputs = []

    def send(towards, src, dst):
        there, device = shifted(*towards)
        back, _ = shifted(*(-v for v in towards))
        index = len(outputs)
        copy = remote(src, dst, send_out.at[index], recv_out.at[index], device)
        outputs.append((copy, there, back))
        pl.when(there)(copy.start)

    def await_out(indices):
        for i in indices:
            copy, _, back = outputs[i]
            pl.when(back)(copy.wait_recv)

    mine[0] = feat[1:5, 1:9, 0:1]
    mine[1] = feat[1:5, 1:9, 63:64]
    send((-1, 0, 0), mine.at[0], rim.at[1, 1:5, 1:9])
    send((1, 0, 0), mine.at[1], rim.at[0, 1:5, 1:9])

    for kz in range(3):
        second[kz, 3, :, 0:128] = jnp.zeros((384, 128), bf16)
        second[kz, 0, :, 128:256] = jnp.zeros((384, 128), bf16)

    phases[0]["middle"](phases[1]["mean"])
    stage[1, column] = phases[0]["total"](float(cells))
    phases[1]["go"]()
    send((0, -1, 0), feat.at[1:5, 1], feat.at[1:5, 9])
    send((0, 1, 0), feat.at[1:5, 8], feat.at[1:5, 0])
    await_out((0, 1))
    send((0, -1, 0), rim.at[:, 1:5, 1], rim.at[:, 1:5, 9])
    send((0, 1, 0), rim.at[:, 1:5, 8], rim.at[:, 1:5, 0])
    phases[1]["middle"](phases[2]["mean"])
    stage[2, gx] = phases[1]["total"](float(cells * group))
    phases[2]["go"]()
    send((0, 0, -1), feat.at[1, 1:9], feat.at[5, 1:9])
    send((0, 0, 1), feat.at[4, 1:9], feat.at[0, 1:9])
    average = phases[2]["middle"](None)
    stage[3, rank] = phases[2]["total"](float(cells * group * columns))
    phases[3]["go"]()
    await_out((2, 3, 4, 5))
    send((0, 0, -1), feat.at[1, 0], feat.at[5, 0])
    send((0, 0, -1), feat.at[1, 9], feat.at[5, 9])
    send((0, 0, 1), feat.at[4, 0], feat.at[0, 0])
    send((0, 0, 1), feat.at[4, 9], feat.at[0, 9])
    send((0, 0, -1), rim.at[:, 1], rim.at[:, 5])
    send((0, 0, 1), rim.at[:, 4], rim.at[:, 0])
    phases[3]["arrive"]()
    await_out((6, 7, 8, 9, 10, 11, 12, 13))
    load_even.wait()
    load_odd.wait()

    summed = stage[3, 0:group].reshape(64, 128)
    half = (lane < 64) == (row < 64)
    eye = (lane == row).astype(f32)
    tiled = jnp.concatenate([summed, summed], axis=0)
    covariance = jnp.where(half, tiled / (cells * nx * ny * nz), 0.0) + EPSILON * eye
    diagonal = jnp.sum(covariance * eye, axis=0, keepdims=True)
    head = iota((1, 128), 1) < 64
    trace_0 = jnp.sum(jnp.where(head, diagonal, 0.0), axis=1, keepdims=True)
    trace_1 = jnp.sum(jnp.where(head, 0.0, diagonal), axis=1, keepdims=True)
    trace = jnp.where(head, trace_0, trace_1)
    scaled = covariance / trace

    def product(a, b):
        a_high, a_low = halves(a)
        b_high, b_low = halves(b)
        return dot(
            jnp.concatenate([a_high, a_low, a_high], axis=1), jnp.concatenate([b_high, b_high, b_low], axis=0)
        )

    def newton_step(newton):
        both = product(newton, jnp.concatenate([newton, scaled], axis=1))
        return 1.5 * newton - 0.5 * product(both[:, :128], both[:, 128:])

    newton = 1.5 * eye - 0.5 * scaled
    for _ in range(NEWTON - 1):
        newton = newton_step(newton)
    mixing = (newton / jnp.sqrt(trace)).T * gain_ref[...]
    mix_high, mix_low = halves(mixing)
    mixer = jnp.concatenate(
        [
            jnp.concatenate([mix_high, mix_low], axis=1),
            jnp.concatenate([mix_high, jnp.zeros((128, 128), bf16)], axis=1),
        ],
        axis=0,
    )

    def activate(block):
        both = dot(jnp.concatenate(halves(block - average), axis=1), mixer)
        value = both[:, :128] + both[:, 128:] + shift_ref[...]
        return jnp.where(value >= 0, value, LEAK * value)

    inside = (gx > 0, gx < nx - 1)
    beyond_y = ((0, has_y), (9, gy < ny - 1))
    beyond_z = {0: has_z, 5: gz < nz - 1}

    def activate_plane(z):
        act = activate(feat[z].reshape(640, 128))
        act = jnp.concatenate(
            [
                jnp.where(beyond_y[0][1], act[0:64], 0.0),
                act[64:576],
                jnp.where(beyond_y[1][1], act[576:640], 0.0),
            ],
            axis=0,
        )
        if z in beyond_z:
            act = jnp.where(beyond_z[z], act, 0.0)
        x = iota((640, 128), 0) % 64
        y = iota((16, 128), 0)
        kept = []
        for side in range(2):
            edge = jnp.concatenate([rim[side, z].reshape(10, 128), jnp.zeros((6, 128), f32)], axis=0)
            keep = inside[side]
            for at, there in beyond_y:
                keep = jnp.logical_and(keep, jnp.logical_or(y != at, there))
            if z in beyond_z:
                keep = jnp.logical_and(keep, beyond_z[z])
            edge = jnp.where(keep, activate(edge), 0.0)[0:10].reshape(10, 1, 128)
            edge = jnp.broadcast_to(edge, (10, 64, 128)).reshape(640, 128)
            turned = pltpu.roll(act, 1 if side == 0 else 639, 0)
            kept.append(jnp.where(x == (0 if side == 0 else 63), edge, turned))
        for at, value in ((0, kept[0]), (128, act), (256, kept[1])):
            value = value.astype(bf16).reshape(5, 2, 64, 128)
            for par in range(2):
                acts[z, par, :, :, at : at + 128] = value[:, par]

    def conv_second_plane(z):
        total = None
        for kz in range(3):
            for s in range(2):
                lhs = jnp.concatenate([acts[z + kz, par, s : s + 4].reshape(256, 384) for par in range(2)], axis=1)
                term = dot(lhs, second[kz, 2 * s : 2 * s + 2].reshape(768, 256))
                total = term if total is None else total + term
        for q in range(4):
            for par in range(2):
                out_ref[z, 2 * q + par] = total[64 * q : 64 * q + 64, 128 * par : 128 * par + 128].astype(bf16)

    activate_plane(0)
    activate_plane(1)
    for z in range(4):
        activate_plane(z + 2)
        conv_second_plane(z)

    for phase in phases:
        phase["finish"]()
    for copy, there, _ in list(inputs.values()) + outputs:
        pl.when(there)(copy.wait_send)


VMEM = pl.BlockSpec(memory_space=pltpu.VMEM)
ANY = pl.BlockSpec(memory_space=pl.ANY)


def body(sizes, field, conv_first, norm_gain, norm_shift, conv_second):
    nx, ny, nz = sizes
    group = ny // 2
    share = 64 // group
    slots = max(group, nx, 2 * nz)
    dma = pltpu.SemaphoreType.DMA
    vmem = pltpu.VMEM
    cells = pl.pallas_call(
        functools.partial(kernel, sizes),
        name="block",
        out_shape=pltpu.VMEM((4, 8, 64, 128), bf16),
        in_specs=[ANY, ANY, VMEM, VMEM, ANY],
        out_specs=VMEM,
        scratch_shapes=[
            vmem((64, 9, 9, 2, 128), bf16),
            vmem((9, 2, 5, 64, 384), bf16),
            vmem((3, 3, 3, 64, 128), bf16),
            vmem((3, 1152, 256), bf16),
            vmem((3, 4, 384, 256), bf16),
            vmem((8, 8, 1, 128), f32),
            vmem((9, 9, 1, 128), f32),
            vmem((8, 64, 128), bf16),
            vmem((9, 64, 128), bf16),
            vmem((6, 10, 64, 128), f32),
            vmem((2, 6, 10, 1, 128), f32),
            vmem((2, 4, 8, 1, 128), f32),
            vmem((6, 2, 5, 64, 384), bf16),
            vmem((group, share, 128), f32),
            vmem((4, slots, share, 128), f32),
            vmem((3, slots, 1, 128), f32),
            vmem((64, 128), f32),
            dma((7,)),
            dma((7,)),
            dma((14,)),
            dma((14,)),
            dma((4, slots)),
            dma((4, slots)),
            dma((3, slots)),
            dma((3, slots)),
            dma((5,)),
            pltpu.SemaphoreType.REGULAR((3,)),
            pltpu.SemaphoreType.REGULAR((3,)),
        ],
        compiler_params=pltpu.CompilerParams(
            collective_id=0, has_side_effects=True, vmem_limit_bytes=60000 * 1024
        ),
    )(
        field.reshape(64, 8, 8, 2, 128),
        conv_first,
        norm_gain.reshape(1, 128),
        norm_shift.reshape(1, 128),
        conv_second.reshape(3, 3, 384, 128),
    )
    return cells.reshape(2048, 128).T.reshape(128, 4, 8, 64)


def solution(mesh):
    sizes = tuple(mesh.shape[a] for a in AXES)
    in_specs = (P(None, "gz", "gy", "gx"), P(), P(), P(), P())
    out_specs = P(None, "gz", "gy", "gx")
    return jax.shard_map(
        functools.partial(body, sizes), mesh=mesh, in_specs=in_specs, out_specs=out_specs, check_vma=False
    )
```
